256 devices in a mesh: ang: 8 (over y, z_hi), tile: 32 (over z_lo, x, core).
Axes of the slice: x: 4, y: 4, z: 8 (z_hi: 2, z_lo: 4; z = z_hi * 4 + z_lo), core: 2. Of those that a mesh axis runs over, the one named last changes fastest.
Arguments:
- phase: float32 [4, 256, 256], P(None, 'tile'), may hold values from -1 to 1
- absorb: float32 [4, 256, 256], P(None, 'tile'), may hold values from 0 to 0.5
- tilts: int32 [512, 2], P(('ang', 'tile')), may hold values from -48 to 47
- windows: int32 [512], P(('ang', 'tile')), may hold values from 0 to 2
- live: int32 [512], P(('ang', 'tile')), may hold values 0 or 1
- measured: bfloat16 [2, 512, 256, 256], P(None, ('ang', 'tile')), may hold values from -24 to 24
Outputs:
- volume_out: float32 [2, 4, 256, 256], P(None, None, 'tile')
- gradient: float32 [2, 4, 256, 256], P(None, None, 'tile')
The draws below stay inside these ranges and needn't reach their ends.
Inputs may be any that keep to these rules, and one draw needn't show every extreme that they name: Angle n passes slices windows[n] and windows[n] + 1. Angle slots with live 0 contribute nothing.
All inputs are finite; a program needn't handle non-finite values. No bound on the sum of `live` on one device may be relied on, other than what follows from the above.
Results may differ from the reference program's by a relative error of at most 0.0046.
Values may be sent and summed in bfloat16 or wider, within the bound.
No kernel may reach another device: no remote copies, remote signals or barrier semaphores. Data moves between devices by JAX's collectives and lax.ppermute only.
A program may use at most 64 MiB of HBM per device.

```python
import math
import jax
import jax.numpy as jnp
from jax import lax

NL = 256
NS = 4
TV_STEPS = 3
NANG = 512


def set_ends(values, own_key, least, largest):
    dims = values.shape
    place = [jax.random.randint(jax.random.fold_in(own_key, axis), (), 0, dims[axis]) for axis in range(len(dims))]
    values = values.at[tuple(place)].set(least)
    longest = dims.index(max(dims))
    place[longest] = (place[longest] + 1) % dims[longest]
    return values.at[tuple(place)].set(largest)


def strengthened(values, rng, source, target, blocks, factor):
    owner, partner = [(jnp.arange(values.shape[axis_at]) // (values.shape[axis_at] // blocks)).reshape([-1 if axis == axis_at else 1 for axis in range(values.ndim)]) for axis_at in (source, target)]
    chosen = jax.random.permutation(rng, blocks)[partner]
    strong = (owner == chosen) | (owner == (partner + blocks // 2) % blocks)
    return jnp.where(strong, factor * values, values)


def block_scale(rng, extent, pieces, low, top_value):
    def one(dim, blocks):
        heights = jax.random.uniform(jax.random.fold_in(jax.random.fold_in(rng, 6), dim), (blocks,), jnp.float32, low / len(pieces), top_value / len(pieces))
        return jnp.repeat(jnp.exp(heights), extent[dim] // blocks).reshape((-1,) + (1,) * (len(extent) - dim - 1))

    loudness = one(*pieces[0])
    for cut in pieces[1:]:
        loudness = loudness * one(*cut)
    return loudness


def bell_draw_with(rng, dims, spread, reach, cuts, heavy, kind=jnp.bfloat16):
    array = spread * jax.random.normal(rng, dims, jnp.float32)
    if cuts:
        array = array * block_scale(rng, dims, cuts, -0.22, 0.18)
    return jnp.clip(strengthened(array, jax.random.fold_in(rng, 3), *heavy), -reach, reach).astype(kind)


def setup_inputs(seed: int = 0) -> dict:
    arg_keys = jax.random.split(jax.random.key(seed), 7)
    return {
        "phase": jnp.clip(jax.random.uniform(arg_keys[0], (NS, NL, NL), jnp.float32, -1.0, 1.0) * block_scale(arg_keys[0], (NS, NL, NL), ((1, 32),), -0.4, 0.0), -1.0, 1.0),
        "absorb": jnp.clip(0.5 * jax.random.uniform(arg_keys[1], (NS, NL, NL), jnp.float32) ** block_scale(arg_keys[1], (NS, NL, NL), ((1, 32),), -0.2, 0.2), 0.0, 0.5),
        "tilts": set_ends(jax.random.randint(arg_keys[2], (NANG, 2), -48, 48), jax.random.fold_in(arg_keys[2], 1), -48, 47).astype(jnp.int32),
        "windows": set_ends(jax.random.randint(arg_keys[3], (NANG,), 0, NS - 1), jax.random.fold_in(arg_keys[3], 1), 0, (NS - 1) - 1).astype(jnp.int32),
        "live": set_ends((jax.random.randint(arg_keys[4], (NANG,), 0, 4) < 3).astype(jnp.int32), jax.random.fold_in(arg_keys[4], 1), 0, 1),
        "measured": bell_draw_with(arg_keys[5], (2, NANG, NL, NL), 1.0, 24.0, ((1, 256),), (1, 2, 256, 6.0)),
    }


LAMBDA_TV = 0.25
TAU_DUAL = 0.5
EPS_HUBER = 0.1
STEP_SIZE = 0.5

def circulant(column, length):
    tiled = jnp.tile(column, length + 1).reshape(length, length + 1)
    return tiled[:, 1:][:, ::-1]

def propagator(length):
    indices = jnp.arange(length, dtype=jnp.int32)
    frequency = jnp.where(indices < length // 2, indices, indices - length).astype(jnp.float32)
    kernel_phase = -(math.pi / length) * frequency * frequency
    phases = (indices[:, None] * indices[None, :] % length).astype(jnp.float32) * (2.0 * math.pi / length)
    cosines = jnp.cos(phases)
    sines = jnp.sin(phases)
    kernel_cos = jnp.cos(kernel_phase)
    kernel_sin = jnp.sin(kernel_phase)
    highest = lax.Precision.HIGHEST
    column_real = (jnp.dot(cosines, kernel_cos, precision=highest) - jnp.dot(sines, kernel_sin, precision=highest)) / length
    column_imag = (jnp.dot(cosines, kernel_sin, precision=highest) + jnp.dot(sines, kernel_cos, precision=highest)) / length
    real_part = circulant(column_real.astype(jnp.bfloat16), length)
    imag_part = circulant(column_imag.astype(jnp.bfloat16), length)
    forward_sweep = jnp.concatenate([jnp.concatenate([real_part, -imag_part], 1), jnp.concatenate([imag_part, real_part], 1)], 0)
    backward_sweep = jnp.concatenate([jnp.concatenate([real_part, imag_part], 1), jnp.concatenate([-imag_part, real_part], 1)], 0)
    return (forward_sweep, backward_sweep)

def apply_left(matrix, real, imag):
    length = real.shape[0]
    stacked = jnp.dot(matrix, jnp.concatenate([real, imag], 0).astype(jnp.bfloat16), preferred_element_type=jnp.float32)
    return (stacked[:length], stacked[length:])

def apply_right(matrix, real, imag):
    length = real.shape[1]
    stacked = jnp.dot(jnp.concatenate([real, imag], 1).astype(jnp.bfloat16), matrix, preferred_element_type=jnp.float32)
    return (stacked[:, :length], stacked[:, length:])

def incident(tilt_rowwise, tilt_column, length):
    indices = jnp.arange(length, dtype=jnp.int32)
    turns = (tilt_rowwise * indices[:, None] + tilt_column * indices[None, :]) % length
    phases = turns.astype(jnp.float32) * (2.0 * math.pi / length)
    return (jnp.cos(phases), jnp.sin(phases))

def single_angle(transmit_factor, forward_sweep, backward_sweep, tilt_rowwise, tilt_column, start_offset, observed_real, observed_imag):
    length = transmit_factor.shape[2]
    block = lax.dynamic_slice_in_dim(transmit_factor, start_offset.astype(jnp.int32), 2, 1).astype(jnp.float32)
    first_real, first_imag = (block[0, 0], block[1, 0])
    second_real, second_imag = (block[0, 1], block[1, 1])
    wave_real, wave_imag = incident(tilt_rowwise, tilt_column, length)
    enter_real = wave_real * first_real - wave_imag * first_imag
    enter_imag = wave_real * first_imag + wave_imag * first_real
    mid_real, mid_imag = apply_left(forward_sweep, enter_real, enter_imag)
    prop_real, prop_imag = apply_right(backward_sweep, mid_real, mid_imag)
    outgoing_real = prop_real * second_real - prop_imag * second_imag
    outgoing_imag = prop_real * second_imag + prop_imag * second_real
    residual_real = outgoing_real - observed_real.astype(jnp.float32)
    residual_imag = outgoing_imag - observed_imag.astype(jnp.float32)
    phase_two = outgoing_real * residual_imag - outgoing_imag * residual_real
    absorb_two = -(outgoing_real * residual_real + outgoing_imag * residual_imag)
    adj_real = second_real * residual_real + second_imag * residual_imag
    adj_imag = second_real * residual_imag - second_imag * residual_real
    half_real, half_imag = apply_left(backward_sweep, adj_real, adj_imag)
    back_real, back_imag = apply_right(forward_sweep, half_real, half_imag)
    phase_one = enter_real * back_imag - enter_imag * back_real
    absorb_one = -(enter_real * back_real + enter_imag * back_imag)
    return jnp.stack([jnp.stack([phase_one, phase_two]), jnp.stack([absorb_one, absorb_two])])

def divergence(dual_rows, dual_cols, above):
    shifted = jnp.concatenate([above, dual_rows[:, :, :-1, :]], 2)
    left = jnp.pad(dual_cols[..., :-1], ((0, 0), (0, 0), (0, 0), (1, 0)))
    return dual_rows - shifted + dual_cols - left

def slopes(primal, below, keep_rows, inside):
    shifted = jnp.concatenate([primal[:, :, 1:, :], below], 2)
    diff_rows = (shifted - primal) * keep_rows
    diff_cols = jnp.pad(primal[..., 1:] - primal[..., :-1], ((0, 0), (0, 0), (0, 0), (0, 1))) * inside
    return (diff_rows, diff_cols)

def dual_update(dual_rows, dual_cols, diff_rows, diff_cols):
    new_rows = (dual_rows + TAU_DUAL * diff_rows) / (1.0 + TAU_DUAL * EPS_HUBER)
    new_cols = (dual_cols + TAU_DUAL * diff_cols) / (1.0 + TAU_DUAL * EPS_HUBER)
    scale = jnp.maximum(1.0, jnp.sqrt(new_rows * new_rows + new_cols * new_cols))
    return (new_rows / scale, new_cols / scale)

def reference(phase, absorb, tilts, windows, live, measured):
    forward_sweep, backward_sweep = propagator(NL)
    decay = jnp.exp(-absorb)
    transmit_factor = jnp.stack([decay * jnp.cos(phase), decay * jnp.sin(phase)]).astype(jnp.bfloat16)

    def visit(total, entry_list):
        tilt_angle, start_offset, active_flag, observed_real, observed_imag = entry_list
        term_list = single_angle(transmit_factor, forward_sweep, backward_sweep, tilt_angle[0], tilt_angle[1], start_offset, observed_real, observed_imag)
        begin = start_offset.astype(jnp.int32)
        current = lax.dynamic_slice_in_dim(total, begin, 2, 1)
        total = lax.dynamic_update_slice_in_dim(total, current + active_flag.astype(jnp.float32) * term_list, begin, 1)
        return (total, None)
    empty = jnp.zeros((2, NS, NL, NL), jnp.float32)
    total, unused = lax.scan(visit, empty, (tilts, windows, live, measured[0], measured[1]))
    gradient = total * (1.0 / math.sqrt(NANG))
    volume = jnp.stack([phase, absorb]) - STEP_SIZE * gradient
    row_ids = jnp.arange(NL, dtype=jnp.int32)
    inside = jnp.ones((NL, 1), jnp.float32)
    keep_rows = (row_ids < NL - 1).astype(jnp.float32)[:, None]
    zero_row = jnp.zeros((2, NS, 1, NL), jnp.float32)
    dual_rows = jnp.zeros_like(volume)
    dual_cols = jnp.zeros_like(volume)
    for repeat in range(TV_STEPS):
        primal = volume + LAMBDA_TV * divergence(dual_rows, dual_cols, zero_row)
        diff_rows, diff_cols = slopes(primal, zero_row, keep_rows, inside)
        dual_rows, dual_cols = dual_update(dual_rows, dual_cols, diff_rows, diff_cols)
    volume_out = volume + LAMBDA_TV * divergence(dual_rows, dual_cols, zero_row)
    return (volume_out, gradient)
```

```python
import math

import jax
import jax.numpy as jnp
from jax import lax
from jax.experimental import pallas as pl
from jax.experimental.pallas import tpu as pltpu
from jax.sharding import Mesh
from jax.sharding import PartitionSpec as P

TV_STEPS = 3


LAMBDA_TV = 0.25
TAU_DUAL = 0.5
EPS_HUBER = 0.1
STEP_SIZE = 0.5

AXES = ("y", "zh", "zl", "x", "c")
SIZES = (4, 2, 4, 4, 2)
ANG = ("y", "zh")
TILE = ("zl", "x", "c")
CHIPS = ("zl", "x")


def swap_cores(value):
    return lax.ppermute(value, "c", [(0, 1), (1, 0)])


def exchange(value, axes):
    return lax.all_to_all(value, axes, split_axis=0, concat_axis=0, tiled=True)


def propagator(length):
    indices = jnp.arange(length, dtype=jnp.int32)
    gaps = indices[:, None] - indices[None, :]
    turns = (gaps * gaps) % (2 * length)
    phases = turns.astype(jnp.float32) * (math.pi / length) - math.pi / 4
    scale = 1.0 / math.sqrt(length)
    real_part = (jnp.cos(phases) * scale).astype(jnp.bfloat16)
    imag_part = (jnp.sin(phases) * scale).astype(jnp.bfloat16)
    forward_sweep = jnp.concatenate(
        [jnp.concatenate([real_part, -imag_part], 1), jnp.concatenate([imag_part, real_part], 1)], 0
    )
    backward_sweep = jnp.concatenate(
        [jnp.concatenate([real_part, imag_part], 1), jnp.concatenate([-imag_part, real_part], 1)], 0
    )
    return (forward_sweep, backward_sweep)


def angles_kernel(
    numbers, own, other, forward, backward, measured, out, first, wide, tall, acc
):
    length = acc.shape[2]
    slots = measured.shape[1]
    core = numbers[0]
    mine_first = core == 0

    def slice_plane(part, level):
        mine = own[:, part, level].astype(jnp.float32)
        theirs = other[:, part, level].astype(jnp.float32)
        upper = jnp.where(mine_first, mine, theirs)
        lower = jnp.where(mine_first, theirs, mine)
        return jnp.stack([upper, lower], 1).reshape(length, length)

    def factor(tilt, axis):
        shape = (length, 1) if axis == 0 else (1, length)
        index = lax.broadcasted_iota(jnp.int32, shape, axis)
        turns = (tilt * index) & (length - 1)
        phases = turns.astype(jnp.float32) * (2.0 * math.pi / length)
        return jnp.cos(phases), jnp.sin(phases)

    def span(slot):
        return slice(slot * length, (slot + 1) * length)

    acc[...] = jnp.zeros_like(acc)
    for slot in range(slots):
        level = numbers[3 + 4 * slot]
        row_cos, row_sin = factor(numbers[1 + 4 * slot], 0)
        col_cos, col_sin = factor(numbers[2 + 4 * slot], 1)
        wave_real = row_cos * col_cos - row_sin * col_sin
        wave_imag = row_cos * col_sin + row_sin * col_cos
        first_real = slice_plane(0, level)
        first_imag = slice_plane(1, level)
        enter_real = wave_real * first_real - wave_imag * first_imag
        enter_imag = wave_real * first_imag + wave_imag * first_real
        first[0, slot] = enter_real
        first[1, slot] = enter_imag
        tall[:length, span(slot)] = enter_real.astype(jnp.bfloat16)
        tall[length:, span(slot)] = enter_imag.astype(jnp.bfloat16)
    middle = jnp.dot(forward[...], tall[...], preferred_element_type=jnp.float32)
    for slot in range(slots):
        wide[span(slot), :length] = middle[:length, span(slot)].astype(jnp.bfloat16)
        wide[span(slot), length:] = middle[length:, span(slot)].astype(jnp.bfloat16)
    spread = jnp.dot(wide[...], backward[...], preferred_element_type=jnp.float32)
    for slot in range(slots):
        level = numbers[3 + 4 * slot]
        active = numbers[4 + 4 * slot].astype(jnp.float32)
        prop_real = spread[span(slot), :length]
        prop_imag = spread[span(slot), length:]
        second_real = slice_plane(0, level + 1)
        second_imag = slice_plane(1, level + 1)
        outgoing_real = prop_real * second_real - prop_imag * second_imag
        outgoing_imag = prop_real * second_imag + prop_imag * second_real
        residual_real = (outgoing_real - measured[0, slot].astype(jnp.float32)) * active
        residual_imag = (outgoing_imag - measured[1, slot].astype(jnp.float32)) * active
        acc[0, level + 1] += outgoing_real * residual_imag - outgoing_imag * residual_real
        acc[1, level + 1] -= outgoing_real * residual_real + outgoing_imag * residual_imag
        adj_real = second_real * residual_real + second_imag * residual_imag
        adj_imag = second_real * residual_imag - second_imag * residual_real
        tall[:length, span(slot)] = adj_real.astype(jnp.bfloat16)
        tall[length:, span(slot)] = adj_imag.astype(jnp.bfloat16)
    half = jnp.dot(backward[...], tall[...], preferred_element_type=jnp.float32)
    for slot in range(slots):
        wide[span(slot), :length] = half[:length, span(slot)].astype(jnp.bfloat16)
        wide[span(slot), length:] = half[length:, span(slot)].astype(jnp.bfloat16)
    back = jnp.dot(wide[...], forward[...], preferred_element_type=jnp.float32)
    for slot in range(slots):
        level = numbers[3 + 4 * slot]
        enter_real = first[0, slot]
        enter_imag = first[1, slot]
        back_real = back[span(slot), :length]
        back_imag = back[span(slot), length:]
        acc[0, level] += enter_real * back_imag - enter_imag * back_real
        acc[1, level] -= enter_real * back_real + enter_imag * back_imag
    columns = out.shape[2]
    blocks = out.shape[3]
    rows = out.shape[4]
    for component in range(2):
        place = jnp.where(core == component, 0, 1)
        for level in range(acc.shape[1]):
            plane = acc[component, level].astype(jnp.bfloat16)
            plane = plane.reshape(blocks, columns, rows, length)
            for column in range(columns):
                out[place, level, column] = plane[:, column]


def angles(numbers, own, other, forward, backward, measured):
    length = measured.shape[-1]
    depth = own.shape[2]
    slots = measured.shape[1]
    strips = own.shape[0]
    zl, x = SIZES[2], SIZES[3]
    vmem = pl.BlockSpec(memory_space=pltpu.VMEM)
    return pl.pallas_call(
        angles_kernel,
        out_shape=jax.ShapeDtypeStruct((2, depth, x, zl, length // strips, length), jnp.bfloat16),
        in_specs=[pl.BlockSpec(memory_space=pltpu.SMEM)] + [vmem] * 5,
        out_specs=vmem,
        scratch_shapes=[
            pltpu.VMEM((2, slots, length, length), jnp.float32),
            pltpu.VMEM((slots * length, 2 * length), jnp.bfloat16),
            pltpu.VMEM((2 * length, slots * length), jnp.bfloat16),
            pltpu.VMEM((2, depth, length, length), jnp.float32),
        ],
        name="angles",
    )(numbers, own, other, forward, backward, measured)


def divergence(dual_rows, dual_cols, above):
    shifted = jnp.concatenate([above, dual_rows[:, :, :-1, :]], 2)
    left = jnp.pad(dual_cols[..., :-1], ((0, 0), (0, 0), (0, 0), (1, 0)))
    return dual_rows - shifted + dual_cols - left


def slopes(primal, below, keep_rows, inside):
    shifted = jnp.concatenate([primal[:, :, 1:, :], below], 2)
    diff_rows = (shifted - primal) * keep_rows
    diff_cols = (
        jnp.pad(primal[..., 1:] - primal[..., :-1], ((0, 0), (0, 0), (0, 0), (0, 1))) * inside
    )
    return (diff_rows, diff_cols)


def dual_update(dual_rows, dual_cols, diff_rows, diff_cols):
    new_rows = (dual_rows + TAU_DUAL * diff_rows) / (1.0 + TAU_DUAL * EPS_HUBER)
    new_cols = (dual_cols + TAU_DUAL * diff_cols) / (1.0 + TAU_DUAL * EPS_HUBER)
    scale = jnp.maximum(1.0, jnp.sqrt(new_rows * new_rows + new_cols * new_cols))
    return (new_rows / scale, new_cols / scale)


def row_masks(first_global, count, length):
    global_rows = first_global + jnp.arange(count, dtype=jnp.int32)
    inside = ((global_rows >= 0) & (global_rows < length)).astype(jnp.float32)
    keep_rows = inside * (global_rows < length - 1).astype(jnp.float32)
    return (keep_rows[:, None], inside[:, None])


def on_device(phase, absorb, tilts, windows, live, measured):
    slots = tilts.shape[0]
    depth, strip, length = phase.shape
    chips = length // (2 * strip)
    core = lax.axis_index("c")

    decay = jnp.exp(-absorb)
    local_trans = jnp.stack([decay * jnp.cos(phase), decay * jnp.sin(phase)]).astype(jnp.bfloat16)
    own = exchange(jnp.broadcast_to(local_trans[None], (chips, *local_trans.shape)), CHIPS)
    other = swap_cores(own)
    params = jnp.stack([phase, absorb])
    partner_params = swap_cores(params)

    forward_sweep, backward_sweep = propagator(length)
    numbers = jnp.concatenate(
        [core[None].astype(jnp.int32), jnp.concatenate([tilts, windows[:, None], live[:, None]], 1).reshape(-1)]
    )
    halves = angles(numbers, own, other, forward_sweep, backward_sweep, measured)

    pair = halves[0].astype(jnp.float32) + swap_cores(halves[1]).astype(jnp.float32)
    y, x = SIZES[0], SIZES[3]
    pair = pair.astype(jnp.bfloat16).reshape(y * x, -1, 2 * strip, length)
    plane = exchange(pair, ("y", "x")).astype(jnp.float32).sum(0).astype(jnp.bfloat16)
    copies = SIZES[0] * SIZES[1]
    sent = jnp.broadcast_to(plane[None], (copies, *plane.shape)).reshape(-1, *plane.shape[1:])
    column = exchange(sent, ("y", "zh", "zl")).astype(jnp.float32)
    column = column.reshape(depth, -1, 2 * strip, length).sum(1)
    all_slots = slots * math.prod(SIZES)
    mine = column * (1.0 / math.sqrt(all_slots))
    theirs = swap_cores(mine)
    both = jnp.stack([jnp.where(core == 0, mine, theirs), jnp.where(core == 0, theirs, mine)])
    upper, lower = both[:, :, :strip], both[:, :, strip:]
    gradient = jnp.where(core == 0, upper, lower)
    partner_gradient = jnp.where(core == 0, lower, upper)
    volume = params - STEP_SIZE * gradient
    partner_volume = partner_params - STEP_SIZE * partner_gradient

    last = volume[:, :, strip - TV_STEPS :]
    head = volume[:, :, :TV_STEPS]
    tiles = SIZES[2] * SIZES[3] * SIZES[4]
    borders = [(i, i + 1) for i in range(1, tiles - 1, 2)]
    borders = borders + [(j, i) for i, j in borders]
    far = lax.ppermute(jnp.where(core == 0, head, last), TILE, borders)
    before = jnp.where(core == 0, far, partner_volume[:, :, strip - TV_STEPS :])
    after = jnp.where(core == 0, partner_volume[:, :, :TV_STEPS], far)
    extended = jnp.concatenate([before, volume, after], 2)

    first_row = lax.axis_index(TILE) * strip
    count = strip + 2 * TV_STEPS
    keep_rows, inside = row_masks(first_row - TV_STEPS, count, length)
    zero_row = jnp.zeros((2, depth, 1, length), jnp.float32)
    dual_rows = jnp.zeros_like(extended)
    dual_cols = jnp.zeros_like(extended)
    for repeat in range(TV_STEPS):
        primal = extended + LAMBDA_TV * divergence(dual_rows, dual_cols, zero_row)
        diff_rows, diff_cols = slopes(primal, zero_row, keep_rows, inside)
        dual_rows, dual_cols = dual_update(dual_rows, dual_cols, diff_rows, diff_cols)
    wide_out = extended + LAMBDA_TV * divergence(dual_rows, dual_cols, zero_row)
    volume_out = wide_out[:, :, TV_STEPS : TV_STEPS + strip, :]
    return (volume_out, gradient)


def solution(mesh):
    fine = Mesh(mesh.devices.reshape(SIZES), AXES)
    slots = (*ANG, *TILE)
    placed = (
        P(None, TILE, None),
        P(None, TILE, None),
        P(slots, None),
        P(slots),
        P(slots),
        P(None, slots, None, None),
    )
    return jax.shard_map(
        on_device,
        mesh=fine,
        in_specs=placed,
        out_specs=(P(None, None, TILE, None), P(None, None, TILE, None)),
        check_vma=False,
    )
```

```python
import math

import jax
import jax.numpy as jnp
from jax import lax
from jax.experimental import pallas as pl
from jax.experimental.pallas import tpu as pltpu
from jax.sharding import Mesh
from jax.sharding import PartitionSpec as P

TV_STEPS = 3


LAMBDA_TV = 0.25
TAU_DUAL = 0.5
EPS_HUBER = 0.1
STEP_SIZE = 0.5

AXES = ("y", "zh", "zl", "x", "c")
SIZES = (4, 2, 4, 4, 2)
ANG = ("y", "zh")
TILE = ("zl", "x", "c")
CHIPS = ("zl", "x")


def swap_cores(value):
    return lax.ppermute(value, "c", [(0, 1), (1, 0)])


def exchange(value, axes):
    return lax.all_to_all(value, axes, split_axis=0, concat_axis=0, tiled=True)


def outgoing_kernel(phase, absorb, out):
    decay = jnp.exp(-absorb[...])
    angle = phase[...]
    real = (decay * jnp.cos(angle)).astype(jnp.bfloat16)
    imag = (decay * jnp.sin(angle)).astype(jnp.bfloat16)
    for chip in range(out.shape[0]):
        out[chip, 0] = real
        out[chip, 1] = imag


def outgoing(phase, absorb, chips):
    vmem = pl.BlockSpec(memory_space=pltpu.VMEM)
    return pl.pallas_call(
        outgoing_kernel,
        out_shape=jax.ShapeDtypeStruct((chips, 2, *phase.shape), jnp.bfloat16),
        in_specs=[vmem] * 2,
        out_specs=vmem,
        compiler_params=pltpu.CompilerParams(vmem_limit_bytes=4 << 20),
        name="transmission",
    )(phase, absorb)


def setup_kernel(tilts, forward, backward, waves):
    slots, _, length, _ = waves.shape
    rows = lax.broadcasted_iota(jnp.int32, (length, length), 0)
    columns = lax.broadcasted_iota(jnp.int32, (length, length), 1)
    gaps = rows - columns
    turns = (gaps * gaps) & (2 * length - 1)
    phases = turns.astype(jnp.float32) * (math.pi / length) - math.pi / 4
    scale = 1.0 / math.sqrt(length)
    real = (jnp.cos(phases) * scale).astype(jnp.bfloat16)
    imag = jnp.sin(phases) * scale
    minus = (-imag).astype(jnp.bfloat16)
    imag = imag.astype(jnp.bfloat16)
    for matrix, upper, lower in ((forward, minus, imag), (backward, imag, minus)):
        matrix[:length, :length] = real
        matrix[:length, length:] = upper
        matrix[length:, :length] = lower
        matrix[length:, length:] = real

    def factor(tilt, axis):
        shape = (length, 1) if axis == 0 else (1, length)
        index = lax.broadcasted_iota(jnp.int32, shape, axis)
        turns = (tilt * index) & (length - 1)
        phases = turns.astype(jnp.float32) * (2.0 * math.pi / length)
        return jnp.cos(phases), jnp.sin(phases)

    for slot in range(slots):
        row_cos, row_sin = factor(tilts[slot, 0], 0)
        col_cos, col_sin = factor(tilts[slot, 1], 1)
        waves[slot, 0] = row_cos * col_cos - row_sin * col_sin
        waves[slot, 1] = row_cos * col_sin + row_sin * col_cos


def setup(tilts, length):
    slots = tilts.shape[0]
    vmem = pl.BlockSpec(memory_space=pltpu.VMEM)
    sweep = jax.ShapeDtypeStruct((2 * length, 2 * length), jnp.bfloat16)
    return pl.pallas_call(
        setup_kernel,
        out_shape=(sweep, sweep, jax.ShapeDtypeStruct((slots, 2, length, length), jnp.float32)),
        in_specs=[pl.BlockSpec(memory_space=pltpu.SMEM)],
        out_specs=(vmem,) * 3,
        compiler_params=pltpu.CompilerParams(vmem_limit_bytes=12 << 20),
        name="sweeps_and_waves",
    )(tilts)


def angles_kernel(
    numbers, own, other, forward, backward, waves, measured, keep, send, first, wide, tall, terms
):
    slots, _, length, _ = waves.shape
    core = numbers[0]
    mine_first = core == 0

    def slice_plane(part, level):
        mine = own[:, part, level].astype(jnp.float32)
        theirs = other[:, part, level].astype(jnp.float32)
        upper = jnp.where(mine_first, mine, theirs)
        lower = jnp.where(mine_first, theirs, mine)
        return jnp.stack([upper, lower], 1).reshape(length, length)

    def span(slot):
        return slice(slot * length, (slot + 1) * length)

    for slot in range(slots):
        level = numbers[1 + 2 * slot]
        wave_real = waves[slot, 0]
        wave_imag = waves[slot, 1]
        first_real = slice_plane(0, level)
        first_imag = slice_plane(1, level)
        enter_real = wave_real * first_real - wave_imag * first_imag
        enter_imag = wave_real * first_imag + wave_imag * first_real
        first[0, slot] = enter_real
        first[1, slot] = enter_imag
        tall[:length, span(slot)] = enter_real.astype(jnp.bfloat16)
        tall[length:, span(slot)] = enter_imag.astype(jnp.bfloat16)
    middle = jnp.dot(forward[...], tall[...], preferred_element_type=jnp.float32)
    for slot in range(slots):
        wide[span(slot), :length] = middle[:length, span(slot)].astype(jnp.bfloat16)
        wide[span(slot), length:] = middle[length:, span(slot)].astype(jnp.bfloat16)
    spread = jnp.dot(wide[...], backward[...], preferred_element_type=jnp.float32)
    for slot in range(slots):
        level = numbers[1 + 2 * slot]
        active = numbers[2 + 2 * slot].astype(jnp.float32)
        prop_real = spread[span(slot), :length]
        prop_imag = spread[span(slot), length:]
        second_real = slice_plane(0, level + 1)
        second_imag = slice_plane(1, level + 1)
        outgoing_real = prop_real * second_real - prop_imag * second_imag
        outgoing_imag = prop_real * second_imag + prop_imag * second_real
        residual_real = (outgoing_real - measured[0, slot].astype(jnp.float32)) * active
        residual_imag = (outgoing_imag - measured[1, slot].astype(jnp.float32)) * active
        terms[0, 3 * slot + 1] = outgoing_real * residual_imag - outgoing_imag * residual_real
        terms[1, 3 * slot + 1] = -(outgoing_real * residual_real + outgoing_imag * residual_imag)
        adj_real = second_real * residual_real + second_imag * residual_imag
        adj_imag = second_real * residual_imag - second_imag * residual_real
        tall[:length, span(slot)] = adj_real.astype(jnp.bfloat16)
        tall[length:, span(slot)] = adj_imag.astype(jnp.bfloat16)
        for component in range(2):
            terms[component, 3 * slot + 2] = jnp.zeros((length, length), jnp.float32)
    half = jnp.dot(backward[...], tall[...], preferred_element_type=jnp.float32)
    for slot in range(slots):
        wide[span(slot), :length] = half[:length, span(slot)].astype(jnp.bfloat16)
        wide[span(slot), length:] = half[length:, span(slot)].astype(jnp.bfloat16)
    back = jnp.dot(wide[...], forward[...], preferred_element_type=jnp.float32)
    for slot in range(slots):
        enter_real = first[0, slot]
        enter_imag = first[1, slot]
        back_real = back[span(slot), :length]
        back_imag = back[span(slot), length:]
        terms[0, 3 * slot] = enter_real * back_imag - enter_imag * back_real
        terms[1, 3 * slot] = -(enter_real * back_real + enter_imag * back_imag)
    depth, columns, blocks, rows, _ = keep.shape
    for out, component in ((keep, core), (send, 1 - core)):
        for level in range(depth):
            plane = None
            for slot in range(slots):
                step = level - numbers[1 + 2 * slot]
                which = jnp.where(step == 0, 0, jnp.where(step == 1, 1, 2))
                part = terms[component, 3 * slot + which]
                plane = part if plane is None else plane + part
            plane = plane.astype(jnp.bfloat16).reshape(blocks, columns, rows, length)
            for column in range(columns):
                out[level, column] = plane[:, column]


def angles(numbers, own, other, forward, backward, waves, measured):
    length = measured.shape[-1]
    depth = own.shape[2]
    slots = measured.shape[1]
    strips = own.shape[0]
    zl, x = SIZES[2], SIZES[3]
    vmem = pl.BlockSpec(memory_space=pltpu.VMEM)
    half = jax.ShapeDtypeStruct((depth, x, zl, length // strips, length), jnp.bfloat16)
    return pl.pallas_call(
        angles_kernel,
        out_shape=(half, half),
        in_specs=[pl.BlockSpec(memory_space=pltpu.SMEM)] + [vmem] * 6,
        out_specs=(vmem, vmem),
        scratch_shapes=[
            pltpu.VMEM((2, slots, length, length), jnp.float32),
            pltpu.VMEM((slots * length, 2 * length), jnp.bfloat16),
            pltpu.VMEM((2 * length, slots * length), jnp.bfloat16),
            pltpu.VMEM((2, 3 * slots, length, length), jnp.float32),
        ],
        compiler_params=pltpu.CompilerParams(vmem_limit_bytes=24 << 20),
        name="angles",
    )(numbers, own, other, forward, backward, waves, measured)


def divergence(dual_rows, dual_cols, above):
    shifted = jnp.concatenate([above, dual_rows[:, :, :-1, :]], 2)
    left = jnp.pad(dual_cols[..., :-1], ((0, 0), (0, 0), (0, 0), (1, 0)))
    return dual_rows - shifted + dual_cols - left


def slopes(primal, below, keep_rows, inside):
    shifted = jnp.concatenate([primal[:, :, 1:, :], below], 2)
    diff_rows = (shifted - primal) * keep_rows
    diff_cols = (
        jnp.pad(primal[..., 1:] - primal[..., :-1], ((0, 0), (0, 0), (0, 0), (0, 1))) * inside
    )
    return (diff_rows, diff_cols)


def dual_update(dual_rows, dual_cols, diff_rows, diff_cols):
    new_rows = (dual_rows + TAU_DUAL * diff_rows) / (1.0 + TAU_DUAL * EPS_HUBER)
    new_cols = (dual_cols + TAU_DUAL * diff_cols) / (1.0 + TAU_DUAL * EPS_HUBER)
    scale = jnp.maximum(1.0, jnp.sqrt(new_rows * new_rows + new_cols * new_cols))
    return (new_rows / scale, new_cols / scale)


def row_masks(first_global, count, length):
    global_rows = first_global + jnp.arange(count, dtype=jnp.int32)
    inside = ((global_rows >= 0) & (global_rows < length)).astype(jnp.float32)
    keep_rows = inside * (global_rows < length - 1).astype(jnp.float32)
    return (keep_rows[:, None], inside[:, None])


def on_device(phase, absorb, tilts, windows, live, measured):
    slots = tilts.shape[0]
    depth, strip, length = phase.shape
    chips = length // (2 * strip)
    core = lax.axis_index("c")

    own = exchange(outgoing(phase, absorb, chips), CHIPS)
    params = jnp.stack([phase, absorb])
    partner_params = swap_cores(params)
    forward_sweep, backward_sweep, waves = setup(tilts, length)
    numbers = jnp.concatenate(
        [core[None].astype(jnp.int32), jnp.stack([windows, live], 1).reshape(-1)]
    )
    own, numbers, forward_sweep, backward_sweep, waves, params, partner_params = lax.optimization_barrier(
        (own, numbers, forward_sweep, backward_sweep, waves, params, partner_params)
    )
    other = swap_cores(own)
    keep, send = angles(numbers, own, other, forward_sweep, backward_sweep, waves, measured)

    pair = keep.astype(jnp.float32) + swap_cores(send).astype(jnp.float32)
    y, x = SIZES[0], SIZES[3]
    pair = pair.astype(jnp.bfloat16).reshape(y * x, -1, 2 * strip, length)
    plane = exchange(pair, ("y", "x")).astype(jnp.float32).sum(0).astype(jnp.bfloat16)
    copies = SIZES[0] * SIZES[1]
    sent = jnp.broadcast_to(plane[None], (copies, *plane.shape)).reshape(-1, *plane.shape[1:])
    column = exchange(sent, ("y", "zh", "zl")).astype(jnp.float32)
    column = column.reshape(depth, -1, 2 * strip, length).sum(1)
    all_slots = slots * math.prod(SIZES)
    mine = column * (1.0 / math.sqrt(all_slots))
    theirs = swap_cores(mine)
    both = jnp.stack([jnp.where(core == 0, mine, theirs), jnp.where(core == 0, theirs, mine)])
    upper, lower = both[:, :, :strip], both[:, :, strip:]
    gradient = jnp.where(core == 0, upper, lower)
    partner_gradient = jnp.where(core == 0, lower, upper)
    volume = params - STEP_SIZE * gradient
    partner_volume = partner_params - STEP_SIZE * partner_gradient

    last = volume[:, :, strip - TV_STEPS :]
    head = volume[:, :, :TV_STEPS]
    tiles = SIZES[2] * SIZES[3] * SIZES[4]
    borders = [(i, i + 1) for i in range(1, tiles - 1, 2)]
    borders = borders + [(j, i) for i, j in borders]
    far = lax.ppermute(jnp.where(core == 0, head, last), TILE, borders)
    before = jnp.where(core == 0, far, partner_volume[:, :, strip - TV_STEPS :])
    after = jnp.where(core == 0, partner_volume[:, :, :TV_STEPS], far)
    extended = jnp.concatenate([before, volume, after], 2)

    first_row = lax.axis_index(TILE) * strip
    count = strip + 2 * TV_STEPS
    keep_rows, inside = row_masks(first_row - TV_STEPS, count, length)
    zero_row = jnp.zeros((2, depth, 1, length), jnp.float32)
    dual_rows = jnp.zeros_like(extended)
    dual_cols = jnp.zeros_like(extended)
    for repeat in range(TV_STEPS):
        primal = extended + LAMBDA_TV * divergence(dual_rows, dual_cols, zero_row)
        diff_rows, diff_cols = slopes(primal, zero_row, keep_rows, inside)
        dual_rows, dual_cols = dual_update(dual_rows, dual_cols, diff_rows, diff_cols)
    wide_out = extended + LAMBDA_TV * divergence(dual_rows, dual_cols, zero_row)
    volume_out = wide_out[:, :, TV_STEPS : TV_STEPS + strip, :]
    return (volume_out, gradient)


def solution(mesh):
    fine = Mesh(mesh.devices.reshape(SIZES), AXES)
    slots = (*ANG, *TILE)
    placed = (
        P(None, TILE, None),
        P(None, TILE, None),
        P(slots, None),
        P(slots),
        P(slots),
        P(None, slots, None, None),
    )
    return jax.shard_map(
        on_device,
        mesh=fine,
        in_specs=placed,
        out_specs=(P(None, None, TILE, None), P(None, None, TILE, None)),
        check_vma=False,
    )
```

```python
import functools
import math

import jax
import jax.numpy as jnp
from jax import lax
from jax.experimental import pallas as pl
from jax.experimental.pallas import tpu as pltpu
from jax.sharding import Mesh
from jax.sharding import PartitionSpec as P

TV_STEPS = 3


LAMBDA_TV = 0.25
TAU_DUAL = 0.5
EPS_HUBER = 0.1
STEP_SIZE = 0.5

AXES = ("y", "zh", "zl", "x", "c")
SIZES = (4, 2, 4, 4, 2)
ANG = ("y", "zh")
TILE = ("zl", "x", "c")
CHIPS = ("zl", "x")


def swap_cores(value):
    return lax.ppermute(value, "c", [(0, 1), (1, 0)])


def exchange(value, axes):
    return lax.all_to_all(value, axes, split_axis=0, concat_axis=0, tiled=True)


def outgoing_kernel(phase, absorb, out):
    decay = jnp.exp(-absorb[...])
    angle = phase[...]
    real = (decay * jnp.cos(angle)).astype(jnp.bfloat16)
    imag = (decay * jnp.sin(angle)).astype(jnp.bfloat16)
    for chip in range(out.shape[0]):
        out[chip, 0] = real
        out[chip, 1] = imag


def outgoing(phase, absorb, chips):
    vmem = pl.BlockSpec(memory_space=pltpu.VMEM)
    return pl.pallas_call(
        outgoing_kernel,
        out_shape=jax.ShapeDtypeStruct((chips, 2, *phase.shape), jnp.bfloat16),
        in_specs=[vmem] * 2,
        out_specs=vmem,
        compiler_params=pltpu.CompilerParams(vmem_limit_bytes=4 << 20),
        name="transmission",
    )(phase, absorb)


def setup_kernel(tilts, forward, backward, waves):
    slots, _, length, _ = waves.shape
    rows = lax.broadcasted_iota(jnp.int32, (length, length), 0)
    columns = lax.broadcasted_iota(jnp.int32, (length, length), 1)
    gaps = rows - columns
    turns = (gaps * gaps) & (2 * length - 1)
    phases = turns.astype(jnp.float32) * (math.pi / length) - math.pi / 4
    scale = 1.0 / math.sqrt(length)
    real = (jnp.cos(phases) * scale).astype(jnp.bfloat16)
    imag = jnp.sin(phases) * scale
    minus = (-imag).astype(jnp.bfloat16)
    imag = imag.astype(jnp.bfloat16)
    for matrix, upper, lower in ((forward, minus, imag), (backward, imag, minus)):
        matrix[:length, :length] = real
        matrix[:length, length:] = upper
        matrix[length:, :length] = lower
        matrix[length:, length:] = real

    def factor(tilt, axis):
        shape = (length, 1) if axis == 0 else (1, length)
        index = lax.broadcasted_iota(jnp.int32, shape, axis)
        turns = (tilt * index) & (length - 1)
        phases = turns.astype(jnp.float32) * (2.0 * math.pi / length)
        return jnp.cos(phases), jnp.sin(phases)

    for slot in range(slots):
        row_cos, row_sin = factor(tilts[slot, 0], 0)
        col_cos, col_sin = factor(tilts[slot, 1], 1)
        waves[slot, 0] = row_cos * col_cos - row_sin * col_sin
        waves[slot, 1] = row_cos * col_sin + row_sin * col_cos


def setup(tilts, length):
    slots = tilts.shape[0]
    vmem = pl.BlockSpec(memory_space=pltpu.VMEM)
    sweep = jax.ShapeDtypeStruct((2 * length, 2 * length), jnp.bfloat16)
    return pl.pallas_call(
        setup_kernel,
        out_shape=(sweep, sweep, jax.ShapeDtypeStruct((slots, 2, length, length), jnp.float32)),
        in_specs=[pl.BlockSpec(memory_space=pltpu.SMEM)],
        out_specs=(vmem,) * 3,
        compiler_params=pltpu.CompilerParams(vmem_limit_bytes=12 << 20),
        name="sweeps_and_waves",
    )(tilts)


def angles_kernel(
    numbers, own, other, forward, backward, waves, measured, keep, send, first, wide, tall, terms
):
    slots, _, length, _ = waves.shape
    core = numbers[0]
    mine_first = core == 0

    def slice_plane(part, level):
        mine = own[:, part, level].astype(jnp.float32)
        theirs = other[:, part, level].astype(jnp.float32)
        upper = jnp.where(mine_first, mine, theirs)
        lower = jnp.where(mine_first, theirs, mine)
        return jnp.stack([upper, lower], 1).reshape(length, length)

    def span(slot):
        return slice(slot * length, (slot + 1) * length)

    for slot in range(slots):
        level = numbers[1 + 2 * slot]
        wave_real = waves[slot, 0]
        wave_imag = waves[slot, 1]
        first_real = slice_plane(0, level)
        first_imag = slice_plane(1, level)
        enter_real = wave_real * first_real - wave_imag * first_imag
        enter_imag = wave_real * first_imag + wave_imag * first_real
        first[0, slot] = enter_real
        first[1, slot] = enter_imag
        tall[:length, span(slot)] = enter_real.astype(jnp.bfloat16)
        tall[length:, span(slot)] = enter_imag.astype(jnp.bfloat16)
    middle = jnp.dot(forward[...], tall[...], preferred_element_type=jnp.float32)
    for slot in range(slots):
        wide[span(slot), :length] = middle[:length, span(slot)].astype(jnp.bfloat16)
        wide[span(slot), length:] = middle[length:, span(slot)].astype(jnp.bfloat16)
    spread = jnp.dot(wide[...], backward[...], preferred_element_type=jnp.float32)
    for slot in range(slots):
        level = numbers[1 + 2 * slot]
        active = numbers[2 + 2 * slot].astype(jnp.float32)
        prop_real = spread[span(slot), :length]
        prop_imag = spread[span(slot), length:]
        second_real = slice_plane(0, level + 1)
        second_imag = slice_plane(1, level + 1)
        outgoing_real = prop_real * second_real - prop_imag * second_imag
        outgoing_imag = prop_real * second_imag + prop_imag * second_real
        residual_real = (outgoing_real - measured[0, slot].astype(jnp.float32)) * active
        residual_imag = (outgoing_imag - measured[1, slot].astype(jnp.float32)) * active
        terms[0, 3 * slot + 1] = outgoing_real * residual_imag - outgoing_imag * residual_real
        terms[1, 3 * slot + 1] = -(outgoing_real * residual_real + outgoing_imag * residual_imag)
        adj_real = second_real * residual_real + second_imag * residual_imag
        adj_imag = second_real * residual_imag - second_imag * residual_real
        tall[:length, span(slot)] = adj_real.astype(jnp.bfloat16)
        tall[length:, span(slot)] = adj_imag.astype(jnp.bfloat16)
        for component in range(2):
            terms[component, 3 * slot + 2] = jnp.zeros((length, length), jnp.float32)
    half = jnp.dot(backward[...], tall[...], preferred_element_type=jnp.float32)
    for slot in range(slots):
        wide[span(slot), :length] = half[:length, span(slot)].astype(jnp.bfloat16)
        wide[span(slot), length:] = half[length:, span(slot)].astype(jnp.bfloat16)
    back = jnp.dot(wide[...], forward[...], preferred_element_type=jnp.float32)
    for slot in range(slots):
        enter_real = first[0, slot]
        enter_imag = first[1, slot]
        back_real = back[span(slot), :length]
        back_imag = back[span(slot), length:]
        terms[0, 3 * slot] = enter_real * back_imag - enter_imag * back_real
        terms[1, 3 * slot] = -(enter_real * back_real + enter_imag * back_imag)
    depth, columns, blocks, _, _ = keep.shape
    strip = own.shape[3]
    near = lax.broadcasted_iota(jnp.int32, (strip, length), 0) < strip // 2
    for out, component in ((keep, core), (send, 1 - core)):
        for level in range(depth):
            plane = None
            for slot in range(slots):
                step = level - numbers[1 + 2 * slot]
                which = jnp.where(step == 0, 0, jnp.where(step == 1, 1, 2))
                part = terms[component, 3 * slot + which]
                plane = part if plane is None else plane + part
            for column in range(columns):
                for block in range(blocks):
                    start = (block * columns + column) * 2 * strip
                    after = (start + 2 * strip) % length
                    before = (start - strip) % length
                    border = jnp.where(
                        near, plane[after : after + strip], plane[before : before + strip]
                    )
                    rows = jnp.concatenate([plane[start : start + 2 * strip], border], 0)
                    out[level, column, block] = rows.astype(jnp.bfloat16)


def angles(numbers, own, other, forward, backward, waves, measured):
    length = measured.shape[-1]
    depth = own.shape[2]
    slots = measured.shape[1]
    zl, x = SIZES[2], SIZES[3]
    vmem = pl.BlockSpec(memory_space=pltpu.VMEM)
    half = jax.ShapeDtypeStruct((depth, x, zl, 3 * own.shape[3], length), jnp.bfloat16)
    return pl.pallas_call(
        angles_kernel,
        out_shape=(half, half),
        in_specs=[pl.BlockSpec(memory_space=pltpu.SMEM)] + [vmem] * 6,
        out_specs=(vmem, vmem),
        scratch_shapes=[
            pltpu.VMEM((2, slots, length, length), jnp.float32),
            pltpu.VMEM((slots * length, 2 * length), jnp.bfloat16),
            pltpu.VMEM((2 * length, slots * length), jnp.bfloat16),
            pltpu.VMEM((2, 3 * slots, length, length), jnp.float32),
        ],
        compiler_params=pltpu.CompilerParams(vmem_limit_bytes=24 << 20),
        name="angles",
    )(numbers, own, other, forward, backward, waves, measured)


def regularize_kernel(numbers, column, params, mine, other, *, norm):
    depth, ring, length = params.shape
    owners = column.shape[0] // depth
    strip = mine.shape[2]
    mine_first = numbers[0] == 0
    index = lax.broadcasted_iota(jnp.int32, (ring, length), 0)
    rows = numbers[numbers.shape[0] - 1] + jnp.where(index < ring - strip // 2, index, index - ring)
    keep_rows = (rows >= 0) & (rows < length - 1)
    columns = lax.broadcasted_iota(jnp.int32, (ring, length), 1)
    keep_cols = columns < length - 1
    inner = columns > 0

    def widened(start, dual_rows, dual_cols):
        above = pltpu.roll(dual_rows, 1, 0)
        left = jnp.where(inner, pltpu.roll(dual_cols, 1, 1), 0.0)
        return start + LAMBDA_TV * (dual_rows - above + dual_cols - left)

    for level in range(depth):
        gradient = column[level * owners].astype(jnp.float32)
        for owner in range(1, owners):
            gradient = gradient + column[level * owners + owner].astype(jnp.float32)
        gradient = gradient * norm
        start = params[level] - STEP_SIZE * gradient
        primal = start
        dual_rows = dual_cols = None
        for repeat in range(TV_STEPS):
            step_rows = jnp.where(keep_rows, pltpu.roll(primal, ring - 1, 0) - primal, 0.0) * TAU_DUAL
            step_cols = jnp.where(keep_cols, pltpu.roll(primal, length - 1, 1) - primal, 0.0) * TAU_DUAL
            if repeat > 0:
                step_rows = dual_rows + step_rows
                step_cols = dual_cols + step_cols
            dual_rows = step_rows / (1.0 + TAU_DUAL * EPS_HUBER)
            dual_cols = step_cols / (1.0 + TAU_DUAL * EPS_HUBER)
            scale = jnp.sqrt(jnp.maximum(1.0, dual_rows * dual_rows + dual_cols * dual_cols))
            dual_rows = dual_rows / scale
            dual_cols = dual_cols / scale
            primal = widened(start, dual_rows, dual_cols)
        for result, value in enumerate((gradient, primal)):
            upper, lower = value[:strip], value[strip : 2 * strip]
            mine[result, level] = jnp.where(mine_first, upper, lower)
            other[result, level] = jnp.where(mine_first, lower, upper)


def regularize(numbers, column, params, norm):
    depth, ring, length = params.shape
    vmem = pl.BlockSpec(memory_space=pltpu.VMEM)
    half = jax.ShapeDtypeStruct((2, depth, ring // 3, length), jnp.float32)
    return pl.pallas_call(
        functools.partial(regularize_kernel, norm=norm),
        out_shape=(half, half),
        in_specs=[pl.BlockSpec(memory_space=pltpu.SMEM), vmem, vmem],
        out_specs=(vmem, vmem),
        compiler_params=pltpu.CompilerParams(vmem_limit_bytes=8 << 20),
        name="regularize",
    )(numbers, column, params)


def on_device(phase, absorb, tilts, windows, live, measured):
    slots = tilts.shape[0]
    depth, strip, length = phase.shape
    chips = length // (2 * strip)
    core = lax.axis_index("c")
    mine_first = core == 0

    own = exchange(outgoing(phase, absorb, chips), CHIPS)
    params = jnp.stack([phase, absorb])
    tiles = 2 * chips
    borders = [(i, i + 1) for i in range(1, tiles - 1, 2)]
    borders = borders + [(j, i) for i, j in borders]
    near = jnp.stack([params, lax.ppermute(params, TILE, borders)])
    here = jnp.where(mine_first, near[:, 0], near[:, 1])
    there = swap_cores(jnp.where(mine_first, near[:, 1], near[:, 0]))
    upper, before = jnp.where(mine_first, here, there)
    lower, after = jnp.where(mine_first, there, here)
    half_strip = jnp.arange(strip)[:, None] < strip // 2
    ring = jnp.concatenate([upper, lower, jnp.where(half_strip, after, before)], 1)
    forward_sweep, backward_sweep, waves = setup(tilts, length)
    first_row = lax.axis_index(CHIPS) * (2 * strip)
    numbers = jnp.concatenate(
        [
            core[None].astype(jnp.int32),
            jnp.stack([windows, live], 1).reshape(-1),
            first_row[None].astype(jnp.int32),
        ]
    )
    own, numbers, forward_sweep, backward_sweep, waves, ring = lax.optimization_barrier(
        (own, numbers, forward_sweep, backward_sweep, waves, ring)
    )
    other = swap_cores(own)
    keep, send = angles(numbers, own, other, forward_sweep, backward_sweep, waves, measured)

    pair = keep.astype(jnp.float32) + swap_cores(send).astype(jnp.float32)
    y, x = SIZES[0], SIZES[3]
    pair = pair.astype(jnp.bfloat16).reshape(y * x, -1, *keep.shape[-2:])
    plane = exchange(pair, ("y", "x")).astype(jnp.float32).sum(0).astype(jnp.bfloat16)
    copies = SIZES[0] * SIZES[1]
    sent = jnp.broadcast_to(plane[None], (copies, *plane.shape)).reshape(-1, *plane.shape[1:])
    column = exchange(sent, ("y", "zh", "zl"))
    all_slots = slots * math.prod(SIZES)
    mine, theirs = regularize(numbers, column, ring, 1.0 / math.sqrt(all_slots))
    theirs = swap_cores(theirs)
    gradient, volume_out = jnp.stack(
        [jnp.where(mine_first, mine, theirs), jnp.where(mine_first, theirs, mine)], 1
    )
    return (volume_out, gradient)


def solution(mesh):
    fine = Mesh(mesh.devices.reshape(SIZES), AXES)
    slots = (*ANG, *TILE)
    placed = (
        P(None, TILE, None),
        P(None, TILE, None),
        P(slots, None),
        P(slots),
        P(slots),
        P(None, slots, None, None),
    )
    return jax.shard_map(
        on_device,
        mesh=fine,
        in_specs=placed,
        out_specs=(P(None, None, TILE, None), P(None, None, TILE, None)),
        check_vma=False,
    )
```

```python
import functools
import math

import jax
import jax.numpy as jnp
from jax import lax
from jax.experimental import pallas as pl
from jax.experimental.pallas import tpu as pltpu
from jax.sharding import Mesh
from jax.sharding import PartitionSpec as P

TV_STEPS = 3


LAMBDA_TV = 0.25
TAU_DUAL = 0.5
EPS_HUBER = 0.1
STEP_SIZE = 0.5

AXES = ("y", "zh", "zl", "x", "c")
SIZES = (4, 2, 4, 4, 2)
ANG = ("y", "zh")
TILE = ("zl", "x", "c")
CHIPS = ("zl", "x")


def swap_cores(value):
    return lax.ppermute(value, "c", [(0, 1), (1, 0)])


def exchange(value, axes):
    return lax.all_to_all(value, axes, split_axis=0, concat_axis=0, tiled=True)


def outgoing_kernel(phase, absorb, out):
    decay = jnp.exp(-absorb[...])
    angle = phase[...]
    real = (decay * jnp.cos(angle)).astype(jnp.bfloat16)
    imag = (decay * jnp.sin(angle)).astype(jnp.bfloat16)
    for chip in range(out.shape[0]):
        out[chip, 0] = real
        out[chip, 1] = imag


def outgoing(phase, absorb, chips):
    vmem = pl.BlockSpec(memory_space=pltpu.VMEM)
    return pl.pallas_call(
        outgoing_kernel,
        out_shape=jax.ShapeDtypeStruct((chips, 2, *phase.shape), jnp.bfloat16),
        in_specs=[vmem] * 2,
        out_specs=vmem,
        compiler_params=pltpu.CompilerParams(vmem_limit_bytes=4 << 20),
        name="transmission",
    )(phase, absorb)


def setup_kernel(tilts, forward, backward, waves):
    slots, _, length, _ = waves.shape
    rows = lax.broadcasted_iota(jnp.int32, (length, length), 0)
    columns = lax.broadcasted_iota(jnp.int32, (length, length), 1)
    gaps = rows - columns
    turns = (gaps * gaps) & (2 * length - 1)
    phases = turns.astype(jnp.float32) * (math.pi / length) - math.pi / 4
    scale = 1.0 / math.sqrt(length)
    real = (jnp.cos(phases) * scale).astype(jnp.bfloat16)
    imag = jnp.sin(phases) * scale
    minus = (-imag).astype(jnp.bfloat16)
    imag = imag.astype(jnp.bfloat16)
    for matrix, upper, lower in ((forward, minus, imag), (backward, imag, minus)):
        matrix[:length, :length] = real
        matrix[:length, length:] = upper
        matrix[length:, :length] = lower
        matrix[length:, length:] = real

    def factor(tilt, axis):
        shape = (length, 1) if axis == 0 else (1, length)
        index = lax.broadcasted_iota(jnp.int32, shape, axis)
        turns = (tilt * index) & (length - 1)
        phases = turns.astype(jnp.float32) * (2.0 * math.pi / length)
        return jnp.cos(phases), jnp.sin(phases)

    for slot in range(slots):
        row_cos, row_sin = factor(tilts[slot, 0], 0)
        col_cos, col_sin = factor(tilts[slot, 1], 1)
        waves[slot, 0] = row_cos * col_cos - row_sin * col_sin
        waves[slot, 1] = row_cos * col_sin + row_sin * col_cos


def setup(tilts, length):
    slots = tilts.shape[0]
    vmem = pl.BlockSpec(memory_space=pltpu.VMEM)
    sweep = jax.ShapeDtypeStruct((2 * length, 2 * length), jnp.bfloat16)
    return pl.pallas_call(
        setup_kernel,
        out_shape=(sweep, sweep, jax.ShapeDtypeStruct((slots, 2, length, length), jnp.float32)),
        in_specs=[pl.BlockSpec(memory_space=pltpu.SMEM)],
        out_specs=(vmem,) * 3,
        compiler_params=pltpu.CompilerParams(vmem_limit_bytes=12 << 20),
        name="sweeps_and_waves",
    )(tilts)


def angles_kernel(
    numbers, own, other, forward, backward, waves, measured, keep, send, first, wide, tall, terms
):
    slots, _, length, _ = waves.shape
    core = numbers[0]
    mine_first = core == 0

    def slice_plane(part, level):
        mine = own[:, part, level].astype(jnp.float32)
        theirs = other[:, part, level].astype(jnp.float32)
        upper = jnp.where(mine_first, mine, theirs)
        lower = jnp.where(mine_first, theirs, mine)
        return jnp.stack([upper, lower], 1).reshape(length, length)

    def span(slot):
        return slice(slot * length, (slot + 1) * length)

    for slot in range(slots):
        level = numbers[1 + 2 * slot]
        wave_real = waves[slot, 0]
        wave_imag = waves[slot, 1]
        first_real = slice_plane(0, level)
        first_imag = slice_plane(1, level)
        enter_real = wave_real * first_real - wave_imag * first_imag
        enter_imag = wave_real * first_imag + wave_imag * first_real
        first[0, slot] = enter_real
        first[1, slot] = enter_imag
        tall[:length, span(slot)] = enter_real.astype(jnp.bfloat16)
        tall[length:, span(slot)] = enter_imag.astype(jnp.bfloat16)
    middle = jnp.dot(forward[...], tall[...], preferred_element_type=jnp.float32)
    for slot in range(slots):
        wide[span(slot), :length] = middle[:length, span(slot)].astype(jnp.bfloat16)
        wide[span(slot), length:] = middle[length:, span(slot)].astype(jnp.bfloat16)
    spread = jnp.dot(wide[...], backward[...], preferred_element_type=jnp.float32)
    for slot in range(slots):
        level = numbers[1 + 2 * slot]
        active = numbers[2 + 2 * slot].astype(jnp.float32)
        prop_real = spread[span(slot), :length]
        prop_imag = spread[span(slot), length:]
        second_real = slice_plane(0, level + 1)
        second_imag = slice_plane(1, level + 1)
        outgoing_real = prop_real * second_real - prop_imag * second_imag
        outgoing_imag = prop_real * second_imag + prop_imag * second_real
        residual_real = (outgoing_real - measured[0, slot].astype(jnp.float32)) * active
        residual_imag = (outgoing_imag - measured[1, slot].astype(jnp.float32)) * active
        terms[0, 3 * slot + 1] = outgoing_real * residual_imag - outgoing_imag * residual_real
        terms[1, 3 * slot + 1] = -(outgoing_real * residual_real + outgoing_imag * residual_imag)
        adj_real = second_real * residual_real + second_imag * residual_imag
        adj_imag = second_real * residual_imag - second_imag * residual_real
        tall[:length, span(slot)] = adj_real.astype(jnp.bfloat16)
        tall[length:, span(slot)] = adj_imag.astype(jnp.bfloat16)
        for component in range(2):
            terms[component, 3 * slot + 2] = jnp.zeros((length, length), jnp.float32)
    half = jnp.dot(backward[...], tall[...], preferred_element_type=jnp.float32)
    for slot in range(slots):
        wide[span(slot), :length] = half[:length, span(slot)].astype(jnp.bfloat16)
        wide[span(slot), length:] = half[length:, span(slot)].astype(jnp.bfloat16)
    back = jnp.dot(wide[...], forward[...], preferred_element_type=jnp.float32)
    for slot in range(slots):
        enter_real = first[0, slot]
        enter_imag = first[1, slot]
        back_real = back[span(slot), :length]
        back_imag = back[span(slot), length:]
        terms[0, 3 * slot] = enter_real * back_imag - enter_imag * back_real
        terms[1, 3 * slot] = -(enter_real * back_real + enter_imag * back_imag)
    depth, columns, blocks, _, _ = keep.shape
    strip = own.shape[3]
    near = lax.broadcasted_iota(jnp.int32, (strip, length), 0) < strip // 2
    for out, component in ((keep, core), (send, 1 - core)):
        for level in range(depth):
            plane = None
            for slot in range(slots):
                step = level - numbers[1 + 2 * slot]
                which = jnp.where(step == 0, 0, jnp.where(step == 1, 1, 2))
                part = terms[component, 3 * slot + which]
                plane = part if plane is None else plane + part
            for column in range(columns):
                for block in range(blocks):
                    start = (block * columns + column) * 2 * strip
                    after = (start + 2 * strip) % length
                    before = (start - strip) % length
                    border = jnp.where(
                        near, plane[after : after + strip], plane[before : before + strip]
                    )
                    rows = jnp.concatenate([plane[start : start + 2 * strip], border], 0)
                    out[level, column, block] = rows.astype(jnp.bfloat16)


def angles(numbers, own, other, forward, backward, waves, measured):
    length = measured.shape[-1]
    depth = own.shape[2]
    slots = measured.shape[1]
    zl, x = SIZES[2], SIZES[3]
    vmem = pl.BlockSpec(memory_space=pltpu.VMEM)
    half = jax.ShapeDtypeStruct((depth, x, zl, 3 * own.shape[3], length), jnp.bfloat16)
    return pl.pallas_call(
        angles_kernel,
        out_shape=(half, half),
        in_specs=[pl.BlockSpec(memory_space=pltpu.SMEM)] + [vmem] * 6,
        out_specs=(vmem, vmem),
        scratch_shapes=[
            pltpu.VMEM((2, slots, length, length), jnp.float32),
            pltpu.VMEM((slots * length, 2 * length), jnp.bfloat16),
            pltpu.VMEM((2 * length, slots * length), jnp.bfloat16),
            pltpu.VMEM((2, 3 * slots, length, length), jnp.float32),
        ],
        compiler_params=pltpu.CompilerParams(vmem_limit_bytes=24 << 20),
        name="angles",
    )(numbers, own, other, forward, backward, waves, measured)


def regularize_kernel(numbers, column, params, mine, other, *, norm):
    depth, ring, length = params.shape
    owners = column.shape[0] // depth
    strip = mine.shape[2]
    mine_first = numbers[0] == 0
    index = lax.broadcasted_iota(jnp.int32, (ring, length), 0)
    rows = numbers[numbers.shape[0] - 1] + jnp.where(index < ring - strip // 2, index, index - ring)
    keep_rows = (rows >= 0) & (rows < length - 1)
    columns = lax.broadcasted_iota(jnp.int32, (ring, length), 1)
    keep_cols = columns < length - 1
    inner = columns > 0

    def widened(start, dual_rows, dual_cols):
        above = pltpu.roll(dual_rows, 1, 0)
        left = jnp.where(inner, pltpu.roll(dual_cols, 1, 1), 0.0)
        return start + LAMBDA_TV * (dual_rows - above + dual_cols - left)

    for level in range(depth):
        gradient = column[level * owners].astype(jnp.float32)
        for owner in range(1, owners):
            gradient = gradient + column[level * owners + owner].astype(jnp.float32)
        gradient = gradient * norm
        start = params[level] - STEP_SIZE * gradient
        primal = start
        dual_rows = dual_cols = None
        for repeat in range(TV_STEPS):
            step_rows = jnp.where(keep_rows, pltpu.roll(primal, ring - 1, 0) - primal, 0.0) * TAU_DUAL
            step_cols = jnp.where(keep_cols, pltpu.roll(primal, length - 1, 1) - primal, 0.0) * TAU_DUAL
            if repeat > 0:
                step_rows = dual_rows + step_rows
                step_cols = dual_cols + step_cols
            dual_rows = step_rows / (1.0 + TAU_DUAL * EPS_HUBER)
            dual_cols = step_cols / (1.0 + TAU_DUAL * EPS_HUBER)
            scale = jnp.sqrt(jnp.maximum(1.0, dual_rows * dual_rows + dual_cols * dual_cols))
            dual_rows = dual_rows / scale
            dual_cols = dual_cols / scale
            primal = widened(start, dual_rows, dual_cols)
        for result, value in enumerate((gradient, primal)):
            upper, lower = value[:strip], value[strip : 2 * strip]
            mine[result, level] = jnp.where(mine_first, upper, lower)
            other[result, level] = jnp.where(mine_first, lower, upper)


def regularize(numbers, column, params, norm):
    depth, ring, length = params.shape
    vmem = pl.BlockSpec(memory_space=pltpu.VMEM)
    half = jax.ShapeDtypeStruct((2, depth, ring // 3, length), jnp.float32)
    return pl.pallas_call(
        functools.partial(regularize_kernel, norm=norm),
        out_shape=(half, half),
        in_specs=[pl.BlockSpec(memory_space=pltpu.SMEM), vmem, vmem],
        out_specs=(vmem, vmem),
        compiler_params=pltpu.CompilerParams(vmem_limit_bytes=8 << 20),
        name="regularize",
    )(numbers, column, params)


def on_device(phase, absorb, tilts, windows, live, measured):
    slots = tilts.shape[0]
    depth, strip, length = phase.shape
    chips = length // (2 * strip)
    core = lax.axis_index("c")
    mine_first = core == 0

    sent = outgoing(phase, absorb, chips)
    sent, tilts = lax.optimization_barrier((sent, tilts))
    own = exchange(sent, CHIPS)
    forward_sweep, backward_sweep, waves = setup(tilts, length)
    phase, absorb, waves = lax.optimization_barrier((phase, absorb, waves))
    params = jnp.stack([phase, absorb])
    tiles = 2 * chips
    borders = [(i, i + 1) for i in range(1, tiles - 1, 2)]
    borders = borders + [(j, i) for i, j in borders]
    near = jnp.stack([params, lax.ppermute(params, TILE, borders)])
    here = jnp.where(mine_first, near[:, 0], near[:, 1])
    there = swap_cores(jnp.where(mine_first, near[:, 1], near[:, 0]))
    upper, before = jnp.where(mine_first, here, there)
    lower, after = jnp.where(mine_first, there, here)
    half_strip = jnp.arange(strip)[:, None] < strip // 2
    ring = jnp.concatenate([upper, lower, jnp.where(half_strip, after, before)], 1)
    first_row = lax.axis_index(CHIPS) * (2 * strip)
    numbers = jnp.concatenate(
        [
            core[None].astype(jnp.int32),
            jnp.stack([windows, live], 1).reshape(-1),
            first_row[None].astype(jnp.int32),
        ]
    )
    own, numbers, forward_sweep, backward_sweep, waves, ring = lax.optimization_barrier(
        (own, numbers, forward_sweep, backward_sweep, waves, ring)
    )
    other = swap_cores(own)
    keep, send = angles(numbers, own, other, forward_sweep, backward_sweep, waves, measured)

    pair = keep.astype(jnp.float32) + swap_cores(send).astype(jnp.float32)
    y, x = SIZES[0], SIZES[3]
    pair = pair.astype(jnp.bfloat16).reshape(y * x, -1, *keep.shape[-2:])
    plane = exchange(pair, ("y", "x")).astype(jnp.float32).sum(0).astype(jnp.bfloat16)
    copies = SIZES[0] * SIZES[1]
    sent = jnp.broadcast_to(plane[None], (copies, *plane.shape)).reshape(-1, *plane.shape[1:])
    column = exchange(sent, ("y", "zh", "zl"))
    all_slots = slots * math.prod(SIZES)
    mine, theirs = regularize(numbers, column, ring, 1.0 / math.sqrt(all_slots))
    theirs = swap_cores(theirs)
    gradient, volume_out = jnp.stack(
        [jnp.where(mine_first, mine, theirs), jnp.where(mine_first, theirs, mine)], 1
    )
    return (volume_out, gradient)


def solution(mesh):
    fine = Mesh(mesh.devices.reshape(SIZES), AXES)
    slots = (*ANG, *TILE)
    placed = (
        P(None, TILE, None),
        P(None, TILE, None),
        P(slots, None),
        P(slots),
        P(slots),
        P(None, slots, None, None),
    )
    return jax.shard_map(
        on_device,
        mesh=fine,
        in_specs=placed,
        out_specs=(P(None, None, TILE, None), P(None, None, TILE, None)),
        check_vma=False,
    )
```

```python
import functools
import math

import jax
import jax.numpy as jnp
from jax import lax
from jax.experimental import pallas as pl
from jax.experimental.pallas import tpu as pltpu
from jax.sharding import Mesh
from jax.sharding import PartitionSpec as P

TV_STEPS = 3


LAMBDA_TV = 0.25
TAU_DUAL = 0.5
EPS_HUBER = 0.1
STEP_SIZE = 0.5

AXES = ("y", "zh", "zl", "x", "c")
SIZES = (4, 2, 4, 4, 2)
ANG = ("y", "zh")
TILE = ("zl", "x", "c")
CHIPS = ("zl", "x")


def swap_cores(value):
    return lax.ppermute(value, "c", [(0, 1), (1, 0)])


def exchange(value, axes):
    return lax.all_to_all(value, axes, split_axis=0, concat_axis=0, tiled=True)


def outgoing_kernel(params, out):
    decay = jnp.exp(-params[1])
    angle = params[0]
    real = (decay * jnp.cos(angle)).astype(jnp.bfloat16)
    imag = (decay * jnp.sin(angle)).astype(jnp.bfloat16)
    for chip in range(out.shape[0]):
        out[chip, 0] = real
        out[chip, 1] = imag


def outgoing(params, chips):
    vmem = pl.BlockSpec(memory_space=pltpu.VMEM)
    return pl.pallas_call(
        outgoing_kernel,
        out_shape=jax.ShapeDtypeStruct((chips, *params.shape), jnp.bfloat16),
        in_specs=[vmem],
        out_specs=vmem,
        compiler_params=pltpu.CompilerParams(vmem_limit_bytes=4 << 20),
        name="transmission",
    )(params)


def setup_kernel(tilts, forward, backward, waves):
    slots, _, length, _ = waves.shape
    rows = lax.broadcasted_iota(jnp.int32, (length, length), 0)
    columns = lax.broadcasted_iota(jnp.int32, (length, length), 1)
    gaps = rows - columns
    turns = (gaps * gaps) & (2 * length - 1)
    phases = turns.astype(jnp.float32) * (math.pi / length) - math.pi / 4
    scale = 1.0 / math.sqrt(length)
    real = (jnp.cos(phases) * scale).astype(jnp.bfloat16)
    imag = jnp.sin(phases) * scale
    minus = (-imag).astype(jnp.bfloat16)
    imag = imag.astype(jnp.bfloat16)
    for matrix, upper, lower in ((forward, minus, imag), (backward, imag, minus)):
        matrix[:length, :length] = real
        matrix[:length, length:] = upper
        matrix[length:, :length] = lower
        matrix[length:, length:] = real

    def factor(tilt, axis):
        shape = (length, 1) if axis == 0 else (1, length)
        index = lax.broadcasted_iota(jnp.int32, shape, axis)
        turns = (tilt * index) & (length - 1)
        phases = turns.astype(jnp.float32) * (2.0 * math.pi / length)
        return jnp.cos(phases), jnp.sin(phases)

    for slot in range(slots):
        row_cos, row_sin = factor(tilts[slot, 0], 0)
        col_cos, col_sin = factor(tilts[slot, 1], 1)
        waves[slot, 0] = row_cos * col_cos - row_sin * col_sin
        waves[slot, 1] = row_cos * col_sin + row_sin * col_cos


def setup(tilts, length):
    slots = tilts.shape[0]
    vmem = pl.BlockSpec(memory_space=pltpu.VMEM)
    sweep = jax.ShapeDtypeStruct((2 * length, 2 * length), jnp.bfloat16)
    return pl.pallas_call(
        setup_kernel,
        out_shape=(sweep, sweep, jax.ShapeDtypeStruct((slots, 2, length, length), jnp.float32)),
        in_specs=[pl.BlockSpec(memory_space=pltpu.SMEM)],
        out_specs=(vmem,) * 3,
        compiler_params=pltpu.CompilerParams(vmem_limit_bytes=12 << 20),
        name="sweeps_and_waves",
    )(tilts)


def angles_kernel(
    numbers, own, other, forward, backward, waves, measured, keep, send, first, wide, tall, terms
):
    slots, _, length, _ = waves.shape
    core = numbers[0]
    mine_first = core == 0

    def slice_plane(part, level):
        mine = own[:, part, level].astype(jnp.float32)
        theirs = other[:, part, level].astype(jnp.float32)
        upper = jnp.where(mine_first, mine, theirs)
        lower = jnp.where(mine_first, theirs, mine)
        return jnp.stack([upper, lower], 1).reshape(length, length)

    def span(slot):
        return slice(slot * length, (slot + 1) * length)

    for slot in range(slots):
        level = numbers[1 + 2 * slot]
        wave_real = waves[slot, 0]
        wave_imag = waves[slot, 1]
        first_real = slice_plane(0, level)
        first_imag = slice_plane(1, level)
        enter_real = wave_real * first_real - wave_imag * first_imag
        enter_imag = wave_real * first_imag + wave_imag * first_real
        first[0, slot] = enter_real
        first[1, slot] = enter_imag
        tall[:length, span(slot)] = enter_real.astype(jnp.bfloat16)
        tall[length:, span(slot)] = enter_imag.astype(jnp.bfloat16)
    middle = jnp.dot(forward[...], tall[...], preferred_element_type=jnp.float32)
    for slot in range(slots):
        wide[span(slot), :length] = middle[:length, span(slot)].astype(jnp.bfloat16)
        wide[span(slot), length:] = middle[length:, span(slot)].astype(jnp.bfloat16)
    spread = jnp.dot(wide[...], backward[...], preferred_element_type=jnp.float32)
    for slot in range(slots):
        level = numbers[1 + 2 * slot]
        active = numbers[2 + 2 * slot].astype(jnp.float32)
        prop_real = spread[span(slot), :length]
        prop_imag = spread[span(slot), length:]
        second_real = slice_plane(0, level + 1)
        second_imag = slice_plane(1, level + 1)
        outgoing_real = prop_real * second_real - prop_imag * second_imag
        outgoing_imag = prop_real * second_imag + prop_imag * second_real
        residual_real = (outgoing_real - measured[0, slot].astype(jnp.float32)) * active
        residual_imag = (outgoing_imag - measured[1, slot].astype(jnp.float32)) * active
        terms[0, 3 * slot + 1] = outgoing_real * residual_imag - outgoing_imag * residual_real
        terms[1, 3 * slot + 1] = -(outgoing_real * residual_real + outgoing_imag * residual_imag)
        adj_real = second_real * residual_real + second_imag * residual_imag
        adj_imag = second_real * residual_imag - second_imag * residual_real
        tall[:length, span(slot)] = adj_real.astype(jnp.bfloat16)
        tall[length:, span(slot)] = adj_imag.astype(jnp.bfloat16)
        for component in range(2):
            terms[component, 3 * slot + 2] = jnp.zeros((length, length), jnp.float32)
    half = jnp.dot(backward[...], tall[...], preferred_element_type=jnp.float32)
    for slot in range(slots):
        wide[span(slot), :length] = half[:length, span(slot)].astype(jnp.bfloat16)
        wide[span(slot), length:] = half[length:, span(slot)].astype(jnp.bfloat16)
    back = jnp.dot(wide[...], forward[...], preferred_element_type=jnp.float32)
    for slot in range(slots):
        enter_real = first[0, slot]
        enter_imag = first[1, slot]
        back_real = back[span(slot), :length]
        back_imag = back[span(slot), length:]
        terms[0, 3 * slot] = enter_real * back_imag - enter_imag * back_real
        terms[1, 3 * slot] = -(enter_real * back_real + enter_imag * back_imag)
    blocks, columns, depth, _, _ = keep.shape
    strip = own.shape[3]
    near = lax.broadcasted_iota(jnp.int32, (strip, length), 0) < strip // 2
    for out, component in ((keep, core), (send, 1 - core)):
        for level in range(depth):
            plane = None
            for slot in range(slots):
                step = level - numbers[1 + 2 * slot]
                which = jnp.where(step == 0, 0, jnp.where(step == 1, 1, 2))
                part = terms[component, 3 * slot + which]
                plane = part if plane is None else plane + part
            for column in range(columns):
                for block in range(blocks):
                    start = (block * columns + column) * 2 * strip
                    after = (start + 2 * strip) % length
                    before = (start - strip) % length
                    border = jnp.where(
                        near, plane[after : after + strip], plane[before : before + strip]
                    )
                    rows = jnp.concatenate([plane[start : start + 2 * strip], border], 0)
                    out[block, column, level] = rows.astype(jnp.bfloat16)


def angles(numbers, own, other, forward, backward, waves, measured):
    length = measured.shape[-1]
    depth = own.shape[2]
    slots = measured.shape[1]
    zl, x = SIZES[2], SIZES[3]
    vmem = pl.BlockSpec(memory_space=pltpu.VMEM)
    half = jax.ShapeDtypeStruct((zl, x, depth, 3 * own.shape[3], length), jnp.bfloat16)
    return pl.pallas_call(
        angles_kernel,
        out_shape=(half, half),
        in_specs=[pl.BlockSpec(memory_space=pltpu.SMEM)] + [vmem] * 6,
        out_specs=(vmem, vmem),
        scratch_shapes=[
            pltpu.VMEM((2, slots, length, length), jnp.float32),
            pltpu.VMEM((slots * length, 2 * length), jnp.bfloat16),
            pltpu.VMEM((2 * length, slots * length), jnp.bfloat16),
            pltpu.VMEM((2, 3 * slots, length, length), jnp.float32),
        ],
        compiler_params=pltpu.CompilerParams(vmem_limit_bytes=24 << 20),
        name="angles",
    )(numbers, own, other, forward, backward, waves, measured)


def regularize_kernel(numbers, column, params, mine, other, *, norm):
    depth, ring, length = params.shape
    parts = column.shape[0] // depth
    strip = mine.shape[2]
    mine_first = numbers[0] == 0
    index = lax.broadcasted_iota(jnp.int32, (ring, length), 0)
    rows = numbers[numbers.shape[0] - 1] + jnp.where(index < ring - strip // 2, index, index - ring)
    keep_rows = (rows >= 0) & (rows < length - 1)
    columns = lax.broadcasted_iota(jnp.int32, (ring, length), 1)
    keep_cols = columns < length - 1
    inner = columns > 0

    def widened(start, dual_rows, dual_cols):
        above = pltpu.roll(dual_rows, 1, 0)
        left = jnp.where(inner, pltpu.roll(dual_cols, 1, 1), 0.0)
        return start + LAMBDA_TV * (dual_rows - above + dual_cols - left)

    for level in range(depth):
        pieces = [column[level * parts + part] for part in range(parts)]
        gradient = jnp.concatenate(pieces, 1).astype(jnp.float32) * norm
        start = params[level] - STEP_SIZE * gradient
        primal = start
        dual_rows = dual_cols = None
        for repeat in range(TV_STEPS):
            step_rows = jnp.where(keep_rows, pltpu.roll(primal, ring - 1, 0) - primal, 0.0) * TAU_DUAL
            step_cols = jnp.where(keep_cols, pltpu.roll(primal, length - 1, 1) - primal, 0.0) * TAU_DUAL
            if repeat > 0:
                step_rows = dual_rows + step_rows
                step_cols = dual_cols + step_cols
            dual_rows = step_rows / (1.0 + TAU_DUAL * EPS_HUBER)
            dual_cols = step_cols / (1.0 + TAU_DUAL * EPS_HUBER)
            scale = jnp.sqrt(jnp.maximum(1.0, dual_rows * dual_rows + dual_cols * dual_cols))
            dual_rows = dual_rows / scale
            dual_cols = dual_cols / scale
            primal = widened(start, dual_rows, dual_cols)
        for result, value in enumerate((gradient, primal)):
            upper, lower = value[:strip], value[strip : 2 * strip]
            mine[result, level] = jnp.where(mine_first, upper, lower)
            other[result, level] = jnp.where(mine_first, lower, upper)


def regularize(numbers, column, params, norm):
    depth, ring, length = params.shape
    vmem = pl.BlockSpec(memory_space=pltpu.VMEM)
    half = jax.ShapeDtypeStruct((2, depth, ring // 3, length), jnp.float32)
    return pl.pallas_call(
        functools.partial(regularize_kernel, norm=norm),
        out_shape=(half, half),
        in_specs=[pl.BlockSpec(memory_space=pltpu.SMEM), vmem, vmem],
        out_specs=(vmem, vmem),
        compiler_params=pltpu.CompilerParams(vmem_limit_bytes=8 << 20),
        name="regularize",
    )(numbers, column, params)


def on_device(phase, absorb, tilts, windows, live, measured):
    slots = tilts.shape[0]
    depth, strip, length = phase.shape
    chips = length // (2 * strip)
    core = lax.axis_index("c")
    mine_first = core == 0

    params = lax.optimization_barrier(jnp.stack([phase, absorb]))
    sent = outgoing(params, chips)
    sent, tilts = lax.optimization_barrier((sent, tilts))
    own = exchange(sent, CHIPS)
    forward_sweep, backward_sweep, waves = setup(tilts, length)
    params, waves = lax.optimization_barrier((params, waves))
    tiles = 2 * chips
    borders = [(i, i + 1) for i in range(1, tiles - 1, 2)]
    borders = borders + [(j, i) for i, j in borders]
    near = jnp.stack([params, lax.ppermute(params, TILE, borders)])
    here = jnp.where(mine_first, near[:, 0], near[:, 1])
    there = swap_cores(jnp.where(mine_first, near[:, 1], near[:, 0]))
    upper, before = jnp.where(mine_first, here, there)
    lower, after = jnp.where(mine_first, there, here)
    half_strip = jnp.arange(strip)[:, None] < strip // 2
    ring = jnp.concatenate([upper, lower, jnp.where(half_strip, after, before)], 1)
    first_row = lax.axis_index(CHIPS) * (2 * strip)
    numbers = jnp.concatenate(
        [
            core[None].astype(jnp.int32),
            jnp.stack([windows, live], 1).reshape(-1),
            first_row[None].astype(jnp.int32),
        ]
    )
    own, numbers, forward_sweep, backward_sweep, waves, ring = lax.optimization_barrier(
        (own, numbers, forward_sweep, backward_sweep, waves, ring)
    )
    other = swap_cores(own)
    keep, send = angles(numbers, own, other, forward_sweep, backward_sweep, waves, measured)

    pair = keep.astype(jnp.float32) + swap_cores(send).astype(jnp.float32)
    pair = pair.astype(jnp.bfloat16).reshape(chips, *keep.shape[2:])
    plane = exchange(pair, CHIPS).astype(jnp.float32).sum(0).astype(jnp.bfloat16)
    copies = SIZES[0] * SIZES[1]
    parts = copies // depth
    pieces = jnp.stack(jnp.split(plane, parts, 2), 1).reshape(copies, plane.shape[1], -1)
    piece = exchange(pieces, ANG).astype(jnp.float32).sum(0).astype(jnp.bfloat16)
    column = exchange(jnp.broadcast_to(piece[None], (copies, *piece.shape)), ANG)
    all_slots = slots * math.prod(SIZES)
    mine, theirs = regularize(numbers, column, ring, 1.0 / math.sqrt(all_slots))
    theirs = swap_cores(theirs)
    gradient, volume_out = jnp.stack(
        [jnp.where(mine_first, mine, theirs), jnp.where(mine_first, theirs, mine)], 1
    )
    return (volume_out, gradient)


def solution(mesh):
    fine = Mesh(mesh.devices.reshape(SIZES), AXES)
    slots = (*ANG, *TILE)
    placed = (
        P(None, TILE, None),
        P(None, TILE, None),
        P(slots, None),
        P(slots),
        P(slots),
        P(None, slots, None, None),
    )
    return jax.shard_map(
        on_device,
        mesh=fine,
        in_specs=placed,
        out_specs=(P(None, None, TILE, None), P(None, None, TILE, None)),
        check_vma=False,
    )
```

```python
import functools
import math

import jax
import jax.numpy as jnp
from jax import lax
from jax.experimental import pallas as pl
from jax.experimental.pallas import tpu as pltpu
from jax.sharding import Mesh
from jax.sharding import PartitionSpec as P

TV_STEPS = 3


LAMBDA_TV = 0.25
TAU_DUAL = 0.5
EPS_HUBER = 0.1
STEP_SIZE = 0.5

AXES = ("y", "zh", "zl", "x", "c")
SIZES = (4, 2, 4, 4, 2)
ANG = ("y", "zh")
TILE = ("zl", "x", "c")
CHIPS = ("zl", "x")


def swap_cores(value):
    return lax.ppermute(value, "c", [(0, 1), (1, 0)])


def exchange(value, axes):
    return lax.all_to_all(value, axes, split_axis=0, concat_axis=0, tiled=True)


def outgoing_kernel(params, out):
    decay = jnp.exp(-params[1])
    angle = params[0]
    real = (decay * jnp.cos(angle)).astype(jnp.bfloat16)
    imag = (decay * jnp.sin(angle)).astype(jnp.bfloat16)
    for chip in range(out.shape[0]):
        out[chip, 0] = real
        out[chip, 1] = imag


def outgoing(params, chips):
    vmem = pl.BlockSpec(memory_space=pltpu.VMEM)
    return pl.pallas_call(
        outgoing_kernel,
        out_shape=jax.ShapeDtypeStruct((chips, *params.shape), jnp.bfloat16),
        in_specs=[vmem],
        out_specs=vmem,
        compiler_params=pltpu.CompilerParams(vmem_limit_bytes=4 << 20),
        name="transmission",
    )(params)


def setup_kernel(tilts, forward, backward, waves):
    slots, _, length, _ = waves.shape
    rows = lax.broadcasted_iota(jnp.int32, (length, length), 0)
    columns = lax.broadcasted_iota(jnp.int32, (length, length), 1)
    gaps = rows - columns
    turns = (gaps * gaps) & (2 * length - 1)
    phases = turns.astype(jnp.float32) * (math.pi / length) - math.pi / 4
    scale = 1.0 / math.sqrt(length)
    real = (jnp.cos(phases) * scale).astype(jnp.bfloat16)
    imag = jnp.sin(phases) * scale
    minus = (-imag).astype(jnp.bfloat16)
    imag = imag.astype(jnp.bfloat16)
    for matrix, upper, lower in ((forward, minus, imag), (backward, imag, minus)):
        matrix[:length, :length] = real
        matrix[:length, length:] = upper
        matrix[length:, :length] = lower
        matrix[length:, length:] = real

    def factor(tilt, axis):
        shape = (length, 1) if axis == 0 else (1, length)
        index = lax.broadcasted_iota(jnp.int32, shape, axis)
        turns = (tilt * index) & (length - 1)
        phases = turns.astype(jnp.float32) * (2.0 * math.pi / length)
        return jnp.cos(phases), jnp.sin(phases)

    for slot in range(slots):
        row_cos, row_sin = factor(tilts[slot, 0], 0)
        col_cos, col_sin = factor(tilts[slot, 1], 1)
        waves[slot, 0] = row_cos * col_cos - row_sin * col_sin
        waves[slot, 1] = row_cos * col_sin + row_sin * col_cos


def setup(tilts, length):
    slots = tilts.shape[0]
    vmem = pl.BlockSpec(memory_space=pltpu.VMEM)
    sweep = jax.ShapeDtypeStruct((2 * length, 2 * length), jnp.bfloat16)
    return pl.pallas_call(
        setup_kernel,
        out_shape=(sweep, sweep, jax.ShapeDtypeStruct((slots, 2, length, length), jnp.float32)),
        in_specs=[pl.BlockSpec(memory_space=pltpu.SMEM)],
        out_specs=(vmem,) * 3,
        compiler_params=pltpu.CompilerParams(vmem_limit_bytes=12 << 20),
        name="sweeps_and_waves",
    )(tilts)


def angles_kernel(
    numbers, own, other, forward, backward, waves, measured, keep, send, first, wide, tall, terms
):
    slots, _, length, _ = waves.shape
    core = numbers[0]
    mine_first = core == 0

    def slice_plane(part, level):
        mine = own[:, part, level].astype(jnp.float32)
        theirs = other[:, part, level].astype(jnp.float32)
        upper = jnp.where(mine_first, mine, theirs)
        lower = jnp.where(mine_first, theirs, mine)
        return jnp.stack([upper, lower], 1).reshape(length, length)

    def span(slot):
        return slice(slot * length, (slot + 1) * length)

    for slot in range(slots):
        level = numbers[1 + 2 * slot]
        wave_real = waves[slot, 0]
        wave_imag = waves[slot, 1]
        first_real = slice_plane(0, level)
        first_imag = slice_plane(1, level)
        enter_real = wave_real * first_real - wave_imag * first_imag
        enter_imag = wave_real * first_imag + wave_imag * first_real
        first[0, slot] = enter_real
        first[1, slot] = enter_imag
        tall[:length, span(slot)] = enter_real.astype(jnp.bfloat16)
        tall[length:, span(slot)] = enter_imag.astype(jnp.bfloat16)
    middle = jnp.dot(forward[...], tall[...], preferred_element_type=jnp.float32)
    for slot in range(slots):
        wide[span(slot), :length] = middle[:length, span(slot)].astype(jnp.bfloat16)
        wide[span(slot), length:] = middle[length:, span(slot)].astype(jnp.bfloat16)
    spread = jnp.dot(wide[...], backward[...], preferred_element_type=jnp.float32)
    for slot in range(slots):
        level = numbers[1 + 2 * slot]
        active = numbers[2 + 2 * slot].astype(jnp.float32)
        prop_real = spread[span(slot), :length]
        prop_imag = spread[span(slot), length:]
        second_real = slice_plane(0, level + 1)
        second_imag = slice_plane(1, level + 1)
        outgoing_real = prop_real * second_real - prop_imag * second_imag
        outgoing_imag = prop_real * second_imag + prop_imag * second_real
        residual_real = (outgoing_real - measured[0, slot].astype(jnp.float32)) * active
        residual_imag = (outgoing_imag - measured[1, slot].astype(jnp.float32)) * active
        terms[0, 3 * slot + 1] = outgoing_real * residual_imag - outgoing_imag * residual_real
        terms[1, 3 * slot + 1] = -(outgoing_real * residual_real + outgoing_imag * residual_imag)
        adj_real = second_real * residual_real + second_imag * residual_imag
        adj_imag = second_real * residual_imag - second_imag * residual_real
        tall[:length, span(slot)] = adj_real.astype(jnp.bfloat16)
        tall[length:, span(slot)] = adj_imag.astype(jnp.bfloat16)
        for component in range(2):
            terms[component, 3 * slot + 2] = jnp.zeros((length, length), jnp.float32)
    half = jnp.dot(backward[...], tall[...], preferred_element_type=jnp.float32)
    for slot in range(slots):
        wide[span(slot), :length] = half[:length, span(slot)].astype(jnp.bfloat16)
        wide[span(slot), length:] = half[length:, span(slot)].astype(jnp.bfloat16)
    back = jnp.dot(wide[...], forward[...], preferred_element_type=jnp.float32)
    for slot in range(slots):
        enter_real = first[0, slot]
        enter_imag = first[1, slot]
        back_real = back[span(slot), :length]
        back_imag = back[span(slot), length:]
        terms[0, 3 * slot] = enter_real * back_imag - enter_imag * back_real
        terms[1, 3 * slot] = -(enter_real * back_real + enter_imag * back_imag)
    depth, columns, blocks, _, _ = keep.shape
    strip = own.shape[3]
    near = lax.broadcasted_iota(jnp.int32, (strip, length), 0) < strip // 2
    for out, component in ((keep, core), (send, 1 - core)):
        for level in range(depth):
            plane = None
            for slot in range(slots):
                step = level - numbers[1 + 2 * slot]
                which = jnp.where(step == 0, 0, jnp.where(step == 1, 1, 2))
                part = terms[component, 3 * slot + which]
                plane = part if plane is None else plane + part
            for column in range(columns):
                for block in range(blocks):
                    start = (block * columns + column) * 2 * strip
                    after = (start + 2 * strip) % length
                    before = (start - strip) % length
                    border = jnp.where(
                        near, plane[after : after + strip], plane[before : before + strip]
                    )
                    rows = jnp.concatenate([plane[start : start + 2 * strip], border], 0)
                    out[level, column, block] = rows.astype(jnp.bfloat16)


def angles(numbers, own, other, forward, backward, waves, measured):
    length = measured.shape[-1]
    depth = own.shape[2]
    slots = measured.shape[1]
    zl, x = SIZES[2], SIZES[3]
    vmem = pl.BlockSpec(memory_space=pltpu.VMEM)
    half = jax.ShapeDtypeStruct((depth, x, zl, 3 * own.shape[3], length), jnp.bfloat16)
    return pl.pallas_call(
        angles_kernel,
        out_shape=(half, half),
        in_specs=[pl.BlockSpec(memory_space=pltpu.SMEM)] + [vmem] * 6,
        out_specs=(vmem, vmem),
        scratch_shapes=[
            pltpu.VMEM((2, slots, length, length), jnp.float32),
            pltpu.VMEM((slots * length, 2 * length), jnp.bfloat16),
            pltpu.VMEM((2 * length, slots * length), jnp.bfloat16),
            pltpu.VMEM((2, 3 * slots, length, length), jnp.float32),
        ],
        compiler_params=pltpu.CompilerParams(vmem_limit_bytes=24 << 20),
        name="angles",
    )(numbers, own, other, forward, backward, waves, measured)


def regularize_kernel(numbers, column, params, mine, other, *, norm):
    depth, ring, length = params.shape
    owners = column.shape[0] // depth
    strip = mine.shape[2]
    mine_first = numbers[0] == 0
    index = lax.broadcasted_iota(jnp.int32, (ring, length), 0)
    rows = numbers[numbers.shape[0] - 1] + jnp.where(index < ring - strip // 2, index, index - ring)
    keep_rows = (rows >= 0) & (rows < length - 1)
    columns = lax.broadcasted_iota(jnp.int32, (ring, length), 1)
    keep_cols = columns < length - 1
    inner = columns > 0

    def widened(start, dual_rows, dual_cols):
        above = pltpu.roll(dual_rows, 1, 0)
        left = jnp.where(inner, pltpu.roll(dual_cols, 1, 1), 0.0)
        return start + LAMBDA_TV * (dual_rows - above + dual_cols - left)

    for level in range(depth):
        gradient = column[level * owners].astype(jnp.float32)
        for owner in range(1, owners):
            gradient = gradient + column[level * owners + owner].astype(jnp.float32)
        gradient = gradient * norm
        start = params[level] - STEP_SIZE * gradient
        primal = start
        dual_rows = dual_cols = None
        for repeat in range(TV_STEPS):
            step_rows = jnp.where(keep_rows, pltpu.roll(primal, ring - 1, 0) - primal, 0.0) * TAU_DUAL
            step_cols = jnp.where(keep_cols, pltpu.roll(primal, length - 1, 1) - primal, 0.0) * TAU_DUAL
            if repeat > 0:
                step_rows = dual_rows + step_rows
                step_cols = dual_cols + step_cols
            dual_rows = step_rows / (1.0 + TAU_DUAL * EPS_HUBER)
            dual_cols = step_cols / (1.0 + TAU_DUAL * EPS_HUBER)
            scale = jnp.sqrt(jnp.maximum(1.0, dual_rows * dual_rows + dual_cols * dual_cols))
            dual_rows = dual_rows / scale
            dual_cols = dual_cols / scale
            primal = widened(start, dual_rows, dual_cols)
        for result, value in enumerate((gradient, primal)):
            upper, lower = value[:strip], value[strip : 2 * strip]
            mine[result, level] = jnp.where(mine_first, upper, lower)
            other[result, level] = jnp.where(mine_first, lower, upper)


def regularize(numbers, column, params, norm):
    depth, ring, length = params.shape
    vmem = pl.BlockSpec(memory_space=pltpu.VMEM)
    half = jax.ShapeDtypeStruct((2, depth, ring // 3, length), jnp.float32)
    return pl.pallas_call(
        functools.partial(regularize_kernel, norm=norm),
        out_shape=(half, half),
        in_specs=[pl.BlockSpec(memory_space=pltpu.SMEM), vmem, vmem],
        out_specs=(vmem, vmem),
        compiler_params=pltpu.CompilerParams(vmem_limit_bytes=8 << 20),
        name="regularize",
    )(numbers, column, params)


def on_device(phase, absorb, tilts, windows, live, measured):
    slots = tilts.shape[0]
    depth, strip, length = phase.shape
    chips = length // (2 * strip)
    core = lax.axis_index("c")
    mine_first = core == 0

    params = lax.optimization_barrier(jnp.stack([phase, absorb]))
    sent = outgoing(params, chips)
    sent, tilts = lax.optimization_barrier((sent, tilts))
    own = exchange(sent, CHIPS)
    forward_sweep, backward_sweep, waves = setup(tilts, length)
    params, waves = lax.optimization_barrier((params, waves))
    tiles = 2 * chips
    borders = [(i, i + 1) for i in range(1, tiles - 1, 2)]
    borders = borders + [(j, i) for i, j in borders]
    near = jnp.stack([params, lax.ppermute(params, TILE, borders)])
    here = jnp.where(mine_first, near[:, 0], near[:, 1])
    there = swap_cores(jnp.where(mine_first, near[:, 1], near[:, 0]))
    upper, before = jnp.where(mine_first, here, there)
    lower, after = jnp.where(mine_first, there, here)
    half_strip = jnp.arange(strip)[:, None] < strip // 2
    ring = jnp.concatenate([upper, lower, jnp.where(half_strip, after, before)], 1)
    first_row = lax.axis_index(CHIPS) * (2 * strip)
    numbers = jnp.concatenate(
        [
            core[None].astype(jnp.int32),
            jnp.stack([windows, live], 1).reshape(-1),
            first_row[None].astype(jnp.int32),
        ]
    )
    own, numbers, forward_sweep, backward_sweep, waves, ring = lax.optimization_barrier(
        (own, numbers, forward_sweep, backward_sweep, waves, ring)
    )
    other = swap_cores(own)
    keep, send = angles(numbers, own, other, forward_sweep, backward_sweep, waves, measured)

    pair = keep.astype(jnp.float32) + swap_cores(send).astype(jnp.float32)
    y, x = SIZES[0], SIZES[3]
    pair = pair.astype(jnp.bfloat16).reshape(y * x, -1, *keep.shape[-2:])
    plane = exchange(pair, ("y", "x")).astype(jnp.float32).sum(0).astype(jnp.bfloat16)
    copies = SIZES[0] * SIZES[1]
    sent = jnp.broadcast_to(plane[None], (copies, *plane.shape)).reshape(-1, *plane.shape[1:])
    column = exchange(sent, ("y", "zh", "zl"))
    all_slots = slots * math.prod(SIZES)
    mine, theirs = regularize(numbers, column, ring, 1.0 / math.sqrt(all_slots))
    theirs = swap_cores(theirs)
    gradient, volume_out = jnp.stack(
        [jnp.where(mine_first, mine, theirs), jnp.where(mine_first, theirs, mine)], 1
    )
    return (volume_out, gradient)


def solution(mesh):
    fine = Mesh(mesh.devices.reshape(SIZES), AXES)
    slots = (*ANG, *TILE)
    placed = (
        P(None, TILE, None),
        P(None, TILE, None),
        P(slots, None),
        P(slots),
        P(slots),
        P(None, slots, None, None),
    )
    return jax.shard_map(
        on_device,
        mesh=fine,
        in_specs=placed,
        out_specs=(P(None, None, TILE, None), P(None, None, TILE, None)),
        check_vma=False,
    )
```
